32 devices in a mesh: row: 8 (over z, y), col: 4 (over x, core).
Axes of the slice: x: 2, y: 2, z: 4, core: 2. Of those that a mesh axis runs over, the one named last changes fastest.
Arguments:
- points: float32 [8, 5120], P(None, ('row', 'col')), may hold values from -6 to 6
- sketch: bfloat16 [5120, 256], P(('row', 'col')), may hold values from -0.625 to 0.625
- rank: int32 [5120], P(('row', 'col')), may hold values from 0 to 5119, each once
- boundary: int32 [1], replicated, may hold values from 1280 to 3840
- scales: float32 [8], replicated, may hold values from 1.5 to 4
Outputs:
- basis: float32 [5120, 256], P(('row', 'col'))
- factor: float32 [256, 256], replicated
The draws below stay inside these ranges and needn't reach their ends.
Inputs may be any that keep to these rules, and one draw needn't show every extreme that they name: `rank`: each tree position appears once.
All inputs are finite; a program needn't handle non-finite values.
Results may differ from the reference program's by a relative error of at most 0.0006.
The reference program's roundings to bfloat16 on the way (of `tile`) count: a program that leaves them out, or rounds other values in their place, can miss the bound.
Values may be sent and summed in bfloat16 or wider, within the bound.
A program may use at most 64 MiB of HBM per device.

```python
import math
import jax
import jax.numpy as jnp
from jax import lax

PTS_DEV = 160
DIMS = 8
RANKS = 256
NPTS = 5120
N_COL = 4


def levels(rng, shape, shards, smallest, top_value):
    gain, own = 1.0, jax.random.fold_in(rng, 6)
    for axis_at, blocks in shards:
        draws = jnp.exp(jax.random.uniform(jax.random.fold_in(own, axis_at), (blocks,), jnp.float32, smallest / len(shards), top_value / len(shards)))
        gain = gain * jnp.repeat(draws, shape[axis_at] // blocks).reshape([-1 if axis == axis_at else 1 for axis in range(len(shape))])
    return gain


def centred(stream_key, extent, scale, bound, shards=(), kind=jnp.bfloat16):
    factor_of = levels(stream_key, extent, shards, -0.22, 0.18) if shards else 1.0
    drawn = jax.random.normal(stream_key, extent, jnp.float32) * scale * factor_of
    return jnp.minimum(jnp.maximum(drawn, -bound), bound).astype(kind)


def setup_inputs(seed: int = 0) -> dict:
    seeds = jax.random.split(jax.random.key(seed), 6)
    points = centred(seeds[0], (DIMS, NPTS), 1.0, 6.0, ((1, 32),), jnp.float32)
    sketch = centred(seeds[1], (NPTS, RANKS), (NPTS // 64) ** -0.5, 0.625, ((0, 32),))
    rank = jax.random.permutation(seeds[2], NPTS).astype(jnp.int32)
    boundary = jax.random.randint(seeds[3], (1,), NPTS // 4, 3 * NPTS // 4 + 1).astype(jnp.int32)
    scales = jnp.clip(jnp.exp(jax.random.uniform(seeds[4], (DIMS,), jnp.float32, math.log(1.5), math.log(4.0))), 1.5, 4.0)
    return dict(points=points, sketch=sketch, rank=rank, boundary=boundary, scales=scales)


def reference(points, sketch, rank, boundary, scales):
    scaled = points / scales[:, None]
    sq = jnp.sum(scaled * scaled, axis=0)
    side = (rank >= boundary[0]).astype(jnp.float32)
    block = PTS_DEV * N_COL
    count = NPTS // block

    def one_block(index):
        start = (index * block).astype(jnp.int32)
        tgt = lax.dynamic_slice_in_dim(scaled, start, block, 1)
        tgt_sq = lax.dynamic_slice_in_dim(sq, start, block, 0)
        tgt_side = lax.dynamic_slice_in_dim(side, start, block, 0)
        inner = lax.dot_general(tgt.astype(jnp.float32), scaled.astype(jnp.float32), (((0,), (0,)), ((), ())), precision=lax.Precision.HIGHEST, preferred_element_type=jnp.float32)
        dist = tgt_sq[:, None] + sq[None, :] - 2.0 * inner
        mask = tgt_side[:, None] + side[None, :] - 2.0 * tgt_side[:, None] * side[None, :]
        tile = (jnp.exp(-0.5 * dist) * mask).astype(jnp.bfloat16)
        return jnp.dot(tile.astype(jnp.float32), sketch.astype(jnp.float32), preferred_element_type=jnp.float32)
    sample = lax.map(one_block, jnp.arange(count, dtype=jnp.int32)).reshape(NPTS, RANKS)
    gram = jnp.dot(sample.T.astype(jnp.float32), sample.astype(jnp.float32), precision=lax.Precision.HIGHEST, preferred_element_type=jnp.float32) / jnp.float32(NPTS)
    shift = 0.1 * jnp.trace(gram) / jnp.float32(RANKS)
    factor = jnp.linalg.cholesky(gram + shift * jnp.eye(RANKS, dtype=jnp.float32))
    basis = jax.scipy.linalg.solve_triangular(factor, sample.T, lower=True).T
    return (basis, factor)
```

```python
import functools

import jax
import jax.numpy as jnp
from jax import lax
from jax.experimental import pallas as pl
from jax.experimental.pallas import tpu as pltpu
from jax.sharding import PartitionSpec as P

HIGHEST = lax.Precision.HIGHEST
FAR = 4992.0
VMEM = pl.BlockSpec(memory_space=pltpu.VMEM)
SMEM = pl.BlockSpec(memory_space=pltpu.SMEM)


def dot(a, b, dims, precision=HIGHEST):
    return lax.dot_general(
        a, b, (dims, ((), ())), precision=precision, preferred_element_type=jnp.float32
    )


def remote(src, dst, send, recv, row, col):
    return pltpu.make_async_remote_copy(
        src_ref=src,
        dst_ref=dst,
        send_sem=send,
        recv_sem=recv,
        device_id=(row, col),
        device_id_type=pl.DeviceIdType.MESH,
    )


def each(start, stop, step):
    def run(index, carry):
        step(index)
        return carry

    lax.fori_loop(start, stop, run, 0)


def thirds(x):
    high = x.astype(jnp.bfloat16).astype(jnp.float32)
    mid = (x - high).astype(jnp.bfloat16).astype(jnp.float32)
    return high, mid, (x - high - mid).astype(jnp.bfloat16).astype(jnp.float32)


def sample_kernel(
    rows, cols, points, tests, rank, boundary, scales, sample, gram, front, back, left,
    square, mate, mine, piece, done,
    s_z, r_z, s_a, r_a, s_b, r_b, s_c, r_c,
    s_mate, r_mate, s_piece, r_piece, s_done, r_done, s_over, r_over,
):
    row, col = lax.axis_index("row"), lax.axis_index("col")
    lines, half = rows // 2, cols // 2
    line, odd = row // 2, row % 2
    spot, parity = col // 2, col % 2
    local = tests.shape[0]
    split = local - back.shape[-2]
    dims = points.shape[0]
    mesh = pl.DeviceIdType.MESH
    above, below = line < lines - 1, line > 0

    def there(l, o, s, p):
        return 2 * l + o, 2 * s + p

    barrier = pltpu.get_barrier_semaphore()

    def greet(l, o, s, p):
        pl.semaphore_signal(barrier, 1, device_id=there(l, o, s, p), device_id_type=mesh)

    @pl.when(above)
    def _():
        greet(line + 1, odd, spot, parity)

    @pl.when(below)
    def _():
        greet(line - 1, odd, spot, parity)

    for k in range(1, half):
        greet(line, odd, (spot + k) % half, parity)
    greet(line, 1 - odd, spot, parity)
    greet(line, odd, spot, 1 - parity)

    index = lax.broadcasted_iota(jnp.int32, points.shape, 0)
    scale = jnp.ones(points.shape, jnp.float32)
    for i in range(dims):
        scale = jnp.where(index == i, scales[i], scale)
    scaled = points[...] / scale
    side = jnp.where(rank[...] >= boundary[0], 1.0, 0.0)
    gap = jnp.zeros((-dims % 8, local), jnp.float32)
    high, mid, low = [jnp.concatenate([part, gap], axis=0) if dims % 8 else part for part in thirds(scaled)]
    norms = list(thirds(-0.5 * jnp.sum(scaled * scaled, axis=0, keepdims=True)))
    ones = [jnp.ones_like(side)] * 3
    info = jnp.concatenate([high, mid, low, side, 1.0 - side] + norms + ones, axis=0)
    wide = jnp.zeros((info.shape[0], tests.shape[1] - local), jnp.float32)
    front[line, odd, parity, spot, :split] = tests[:split]
    front[line, odd, parity, spot, split:] = jnp.concatenate([info, wide], axis=1).astype(jnp.bfloat16)
    back[line, spot, parity, odd] = tests[split:]
    left[...] = jnp.concatenate(
        [high, high, mid, mid, low, jnp.zeros_like(low), high, -FAR * side, -FAR * (1.0 - side)] + ones + norms, axis=0
    ).T.astype(jnp.bfloat16)
    sample[...] = jnp.zeros_like(sample)
    near = above.astype(jnp.int32) + below.astype(jnp.int32)
    pl.semaphore_wait(barrier, half + 1 + near)

    def part(c, l):
        return back.at[l, spot, parity, odd] if c else front.at[l, odd, parity, spot]

    def pair(c, l):
        return back.at[l, spot, parity] if c else front.at[l, odd, parity]

    def along(c, l, down):
        return remote(part(c, l), part(c, l), s_z.at[c, down, l], r_z.at[c, l], *there(line + 1 - 2 * down, odd, spot, parity))

    def to_mate(ref, send, recv):
        return remote(ref, ref, send, recv, *there(line, 1 - odd, spot, parity))

    def to_spot(ref, k, send, recv):
        return remote(ref, ref, send, recv, *there(line, odd, (spot + k) % half, parity))

    def hop(c, l):
        if c:
            return [to_mate(part(1, l), s_a.at[1, l, 0], r_a.at[1, l, 0])]
        return [to_spot(part(0, l), k, s_a.at[0, l, k], r_a.at[0, l, k]) for k in range(1, half)]

    def leap(c, l):
        if c:
            return [to_spot(pair(1, l), k, s_b.at[1, l, k], r_b.at[1, l, k]) for k in range(1, half)]
        return [to_mate(pair(0, l), s_b.at[0, l, 0], r_b.at[0, l, 0])]

    def cross(c, l, j):
        ref = back.at[l, j, parity] if c else front.at[l, j, parity]
        return remote(ref, ref, s_c.at[c, l, j], r_c.at[c, l, j], *there(line, odd, spot, 1 - parity))

    def go(copies):
        for copy in copies:
            copy.start()

    def come(copies):
        for copy in copies:
            copy.wait_recv()

    def leave(copies):
        for copy in copies:
            copy.wait_send()

    reach = jnp.minimum(line, lines - 1 - line)
    far = jnp.where(line < lines - 1 - line, 1, -1)

    def origin(n):
        return line + jnp.where(n <= 2 * reach, (2 * (n % 2) - 1) * ((n + 1) // 2), far * (n - reach))

    def upward(l):
        return (l <= line) & above

    def downward(l):
        return (l >= line) & below

    def arrive(n, own=False):
        l = origin(n)
        for c in range(2):
            if not own:
                along(c, l, 0).wait_recv()
            pl.when(upward(l))(along(c, l, 0).start)
            pl.when(downward(l))(along(c, l, 1).start)
            go(hop(c, l))

    def meet(n):
        l = origin(n)
        for c in range(2):
            come(hop(c, l))
            go(leap(c, l))
            cross(c, l, spot if c else odd).start()

    def add(l, p):
        terms = []
        for o in range(2):
            for s in range(half):
                pack = front[l, o, p, s]
                body, head, foot = pack[:split], pack[split : split + 16, :local], pack[split + 16 :, :local]
                right = jnp.concatenate([head, head, head, foot], axis=0)
                tile = jnp.exp(dot(left[...], right, ((1,), (0,)), None)).astype(jnp.bfloat16)
                test = jnp.concatenate([body, back[l, s, p, o]], axis=0)
                terms.append(dot(tile, test, ((1,), (0,)), None))
        while len(terms) > 1:
            terms = [a + b for a, b in zip(terms[::2], terms[1::2])] + terms[len(terms) // 2 * 2 :]
        sample[...] += terms[0]

    def close(n):
        l = origin(n)
        come(leap(0, l))
        cross(0, l, 1 - odd).start()
        for k, copy in enumerate(leap(1, l), 1):
            copy.wait_recv()
            cross(1, l, (spot + half - k) % half).start()
        add(l, parity)

    def last(n):
        l = origin(n)
        come([cross(0, l, j) for j in range(2)] + [cross(1, l, j) for j in range(half)])
        add(l, 1 - parity)

    arrive(0, True)
    meet(0)
    each(1, lines, arrive)

    def turn(n):
        meet(n)
        close(n - 1)
        last(n - 1)

    each(1, lines, turn)
    close(lines - 1)
    last(lines - 1)

    def settle(l):
        for c in range(2):
            pl.when(upward(l))(along(c, l, 0).wait_send)
            pl.when(downward(l))(along(c, l, 1).wait_send)
            leave(hop(c, l) + leap(c, l))
        leave([cross(0, l, j) for j in range(2)] + [cross(1, l, j) for j in range(half)])

    each(0, lines, settle)

    count = rows * half
    partner = col + 1 - 2 * parity
    total = sample[...]
    index = row * half + spot

    def place(i):
        return i // half, 2 * (i % half) + parity

    square[...] = dot(total.T, total, ((1,), (0,))).reshape(square.shape)
    trade = remote(square.at[1 - parity], mate, s_mate.at[0], r_mate.at[0], row, partner)
    trade.start()
    trade.wait()
    mine[...] = square[parity] + mate[...]

    def scatter(k):
        there = (index + k) % count
        r, c = place(there)
        return remote(mine.at[there], piece.at[k], s_piece.at[k], r_piece.at[k], r, c)

    each(1, count, lambda k: scatter(k).start())
    each(1, count, lambda k: scatter(k).wait())
    piece[0] = mine[index]
    done[...] = jnp.sum(piece[...], axis=0)
    gram[parity, index] = done[...]

    def collect(k):
        r, c = place((index + k) % count)
        return remote(done, gram.at[parity, index], s_done.at[k], r_done.at[k], r, c)

    def pass_on(k):
        there = (index + count - k) % count
        return remote(gram.at[parity, there], gram.at[parity, there], s_over.at[k], r_over.at[k], row, partner)

    def relay(k):
        collect(k).wait_recv()
        pass_on(k).start()

    own = remote(done, gram.at[parity, index], s_over.at[0], r_over.at[0], row, partner)
    each(1, count, lambda k: collect(k).start())
    own.start()
    each(1, count, relay)
    own.wait()
    each(1, count, lambda k: pass_on(k).wait())
    each(1, count, lambda k: collect(k).wait_send())


def sketch_gram(points, tests, rank, boundary, scales, rows, cols):
    local, ranks = tests.shape
    lines, half, count = rows // 2, cols // 2, rows * cols // 2
    lanes = 3 * (8 * ((points.shape[0] + 7) // 8)) + 8
    split = (local - lanes) // 32 * 16
    share = ranks // 2 // count
    f32 = jnp.float32
    dma = pltpu.SemaphoreType.DMA
    wide = max(2, half)
    sample, gram = pl.pallas_call(
        functools.partial(sample_kernel, rows, cols),
        out_shape=(
            jax.ShapeDtypeStruct((local, ranks), f32),
            jax.ShapeDtypeStruct((2, count, share, ranks), f32),
        ),
        in_specs=[VMEM, VMEM, VMEM, SMEM, SMEM],
        out_specs=(VMEM, VMEM),
        scratch_shapes=[
            pltpu.VMEM((lines, 2, 2, half, split + lanes, ranks), tests.dtype),
            pltpu.VMEM((lines, half, 2, 2, local - split, ranks), tests.dtype),
            pltpu.VMEM((local, 2 * lanes), tests.dtype),
            pltpu.VMEM((2, count, share, ranks), f32),
            pltpu.VMEM((count, share, ranks), f32),
            pltpu.VMEM((count, share, ranks), f32),
            pltpu.VMEM((count, share, ranks), f32),
            pltpu.VMEM((share, ranks), f32),
            dma((2, 2, lines)), dma((2, lines)),
            dma((2, lines, wide)), dma((2, lines, wide)),
            dma((2, lines, wide)), dma((2, lines, wide)),
            dma((2, lines, wide)), dma((2, lines, wide)),
            dma((1,)), dma((1,)), dma((count,)), dma((count,)), dma((count,)), dma((count,)), dma((count,)), dma((count,)),
        ],
        compiler_params=pltpu.CompilerParams(collective_id=0, has_side_effects=True),
        name="sketch_gram",
    )(points, tests, rank[None], boundary, scales)
    return sample, gram.reshape(ranks, ranks)


def factor_block(a):
    size, wide = a.shape[0], 8
    shape = (wide, size)
    lane = lax.broadcasted_iota(jnp.int32, shape, 1)
    line = lax.broadcasted_iota(jnp.int32, shape, 0)

    def spread(x):
        return jnp.broadcast_to(x, shape)

    blocks = [a[i : i + wide] for i in range(0, size, wide)]
    upper, inverse = [], []
    for b in range(size // wide):
        at = b * wide
        inside = (lane >= at) & (lane < at + wide)
        x = blocks[b]
        y = jnp.where(inside, jnp.where(lane - at == line, 1.0, 0.0), x)
        marks = [spread(x[:, at + u : at + u + 1]) for u in range(wide)]
        over, root = jnp.zeros(shape, jnp.float32), jnp.zeros(shape, jnp.float32)
        for s in range(wide):
            pivot = spread(marks[s][s : s + 1])
            inv = 1.0 / pivot
            over = jnp.where(line == s, inv, over)
            root = jnp.where(line == s, pivot, root)
            if s + 1 < wide:
                low = jnp.where(line > s, marks[s] * inv, 0.0)
                for u in range(s + 1, wide):
                    marks[u] = marks[u] - low * spread(marks[u][s : s + 1])
                x = x - low * spread(x[s : s + 1])
                y = y - low * spread(y[s : s + 1])
        z = y * over
        for s in range(wide - 1, 0, -1):
            z = z - jnp.where(line < s, marks[s] * over, 0.0) * spread(z[s : s + 1])
        rows = [spread(z[t : t + 1]) for t in range(wide)]
        for i in range(b + 1, size // wide):
            old = blocks[i]
            parts = [spread(old[:, at + t : at + t + 1]) * rows[t] for t in range(wide)]
            while len(parts) > 1:
                parts = [p + q for p, q in zip(parts[::2], parts[1::2])]
            blocks[i] = jnp.where(inside, 0.0, old) - parts[0]
        root = lax.rsqrt(root)
        upper.append(jnp.where(lane >= at + line, x * root, 0.0))
        inverse.append(jnp.where(lane <= at + line, y * root, 0.0))
    return jnp.concatenate(upper, axis=0), jnp.concatenate(inverse, axis=0)


def finish_kernel(scale, gram, sample, basis, factor, up, low):
    ranks = gram.shape[0]
    half = ranks // 2
    mean = gram[...] * scale
    same = lax.broadcasted_iota(jnp.int32, (ranks, ranks), 0) == lax.broadcasted_iota(jnp.int32, (ranks, ranks), 1)
    trace = jnp.sum(jnp.sum(jnp.where(same, mean, 0.0), axis=1, keepdims=True), axis=0, keepdims=True)
    factor[...] = jnp.where(same, mean + (0.1 / ranks) * trace, mean)
    cross = factor[:half, half:]

    def one(index):
        start = pl.multiple_of(index * half, half)
        block = factor[pl.ds(start, half), pl.ds(start, half)]
        u, m = factor_block(block)
        up[index] = u
        low[index] = m

        @pl.when(index == 0)
        def _():
            lift = dot(m, cross, ((1,), (0,)))
            up[2] = lift
            factor[half:, half:] = factor[half:, half:] - dot(lift.T, lift, ((1,), (0,)))

    each(0, 2, one)
    lift = up[2]
    first = dot(sample[:, :half], low[0], ((1,), (1,)))
    second = dot(sample[:, half:] - dot(first, lift, ((1,), (0,))), low[1], ((1,), (1,)))
    basis[:, :half] = first
    basis[:, half:] = second
    factor[:half, :half] = up[0].T
    factor[:half, half:] = jnp.zeros((half, half), jnp.float32)
    factor[half:, :half] = lift.T
    factor[half:, half:] = up[1].T


def finish(gram, sample, everyone):
    ranks = gram.shape[0]
    half = ranks // 2
    return pl.pallas_call(
        functools.partial(finish_kernel, 1.0 / everyone),
        out_shape=(
            jax.ShapeDtypeStruct(sample.shape, jnp.float32),
            jax.ShapeDtypeStruct(gram.shape, jnp.float32),
        ),
        in_specs=[VMEM, VMEM],
        out_specs=(VMEM, VMEM),
        scratch_shapes=[pltpu.VMEM((3, half, half), jnp.float32), pltpu.VMEM((2, half, half), jnp.float32)],
        name="finish",
    )(gram, sample)


def body(rows, cols, points, sketch, rank, boundary, scales):
    sample, gram = sketch_gram(points, sketch, rank, boundary, scales, rows, cols)
    return finish(gram, sample, rows * cols * points.shape[1])


def solution(mesh):
    placed = (P(None, ("row", "col")), P(("row", "col"), None), P(("row", "col")), P(), P())
    return jax.shard_map(
        functools.partial(body, mesh.shape["row"], mesh.shape["col"]),
        mesh=mesh,
        in_specs=placed,
        out_specs=(P(("row", "col"), None), P()),
        check_vma=False,
    )
```

```python
import functools

import jax
import jax.numpy as jnp
from jax import lax
from jax.experimental import pallas as pl
from jax.experimental.pallas import tpu as pltpu
from jax.sharding import PartitionSpec as P

HIGHEST = lax.Precision.HIGHEST
FAR = 4992.0
VMEM = pl.BlockSpec(memory_space=pltpu.VMEM)
SMEM = pl.BlockSpec(memory_space=pltpu.SMEM)


def dot(a, b, dims, precision=HIGHEST):
    return lax.dot_general(
        a, b, (dims, ((), ())), precision=precision, preferred_element_type=jnp.float32
    )


def remote(src, dst, send, recv, row, col):
    return pltpu.make_async_remote_copy(
        src_ref=src,
        dst_ref=dst,
        send_sem=send,
        recv_sem=recv,
        device_id=(row, col),
        device_id_type=pl.DeviceIdType.MESH,
    )


def each(start, stop, step):
    def run(index, carry):
        step(index)
        return carry

    lax.fori_loop(start, stop, run, 0)


def thirds(x):
    high = x.astype(jnp.bfloat16).astype(jnp.float32)
    mid = (x - high).astype(jnp.bfloat16).astype(jnp.float32)
    return high, mid, (x - high - mid).astype(jnp.bfloat16).astype(jnp.float32)


def sample_kernel(
    rows, cols, points, tests, rank, boundary, scales, sample, gram, front, back, left,
    square, mate, mine, piece, done,
    s_z, r_z, s_a, r_a, s_b, r_b, s_c, r_c,
    s_mate, r_mate, s_piece, r_piece, s_done, r_done, s_over, r_over,
):
    row, col = lax.axis_index("row"), lax.axis_index("col")
    lines, half = rows // 2, cols // 2
    line, odd = row // 2, row % 2
    spot, parity = col // 2, col % 2
    local = tests.shape[0]
    split = local - back.shape[-2]
    dims = points.shape[0]
    mesh = pl.DeviceIdType.MESH
    above, below = line < lines - 1, line > 0

    def there(l, o, s, p):
        return 2 * l + o, 2 * s + p

    barrier = pltpu.get_barrier_semaphore()

    def greet(l, o, s, p):
        pl.semaphore_signal(barrier, 1, device_id=there(l, o, s, p), device_id_type=mesh)

    @pl.when(above)
    def _():
        greet(line + 1, odd, spot, parity)

    @pl.when(below)
    def _():
        greet(line - 1, odd, spot, parity)

    for k in range(1, half):
        greet(line, odd, (spot + k) % half, parity)
    greet(line, 1 - odd, spot, parity)
    greet(line, odd, spot, 1 - parity)

    index = lax.broadcasted_iota(jnp.int32, points.shape, 0)
    scale = jnp.ones(points.shape, jnp.float32)
    for i in range(dims):
        scale = jnp.where(index == i, scales[i], scale)
    scaled = points[...] / scale
    side = jnp.where(rank[...] >= boundary[0], 1.0, 0.0)
    gap = jnp.zeros((-dims % 8, local), jnp.float32)
    high, mid, low = [jnp.concatenate([part, gap], axis=0) if dims % 8 else part for part in thirds(scaled)]
    norms = list(thirds(-0.5 * jnp.sum(scaled * scaled, axis=0, keepdims=True)))
    ones = [jnp.ones_like(side)] * 3
    info = jnp.concatenate([high, mid, low, side, 1.0 - side] + norms + ones, axis=0)
    wide = jnp.zeros((info.shape[0], tests.shape[1] - local), jnp.float32)
    front[line, odd, parity, spot, :split] = tests[:split]
    front[line, odd, parity, spot, split:] = jnp.concatenate([info, wide], axis=1).astype(jnp.bfloat16)
    back[line, spot, parity, odd] = tests[split:]
    left[...] = jnp.concatenate(
        [high, high, mid, mid, low, jnp.zeros_like(low), high, -FAR * side, -FAR * (1.0 - side)] + ones + norms, axis=0
    ).T.astype(jnp.bfloat16)
    sample[...] = jnp.zeros_like(sample)
    pl.semaphore_wait(barrier, half + 1 + above.astype(jnp.int32) + below.astype(jnp.int32))

    def part(c, l):
        return back.at[l, spot, parity, odd] if c else front.at[l, odd, parity, spot]

    def along(c, l, down):
        return remote(part(c, l), part(c, l), s_z.at[c, down, l], r_z.at[c, l], *there(line + 1 - 2 * down, odd, spot, parity))

    def to_mate(ref, send, recv):
        return remote(ref, ref, send, recv, *there(line, 1 - odd, spot, parity))

    def to_spot(ref, k, send, recv):
        return remote(ref, ref, send, recv, *there(line, odd, (spot + k) % half, parity))

    def hop(c, l):
        if c:
            return [to_mate(part(1, l), s_a.at[1, l, 0], r_a.at[1, l, 0])]
        return [to_spot(part(0, l), k, s_a.at[0, l, k], r_a.at[0, l, k]) for k in range(1, half)]

    def leap(c, l, k):
        if c:
            return [
                to_spot(back.at[l, spot, parity, (odd + k) % 2], j, s_b.at[1, l, k, j], r_b.at[1, l, k, j])
                for j in range(1, half)
            ]
        return [to_mate(front.at[l, odd, parity, (spot + half - k) % half], s_b.at[0, l, k, 0], r_b.at[0, l, k, 0])]

    def leaps(c, l):
        return [copy for k in range(2 if c else half) for copy in leap(c, l, k)]

    def cross(c, l, j):
        ref = back.at[l, j, parity] if c else front.at[l, j, parity]
        return remote(ref, ref, s_c.at[c, l, j], r_c.at[c, l, j], *there(line, odd, spot, 1 - parity))

    def go(copies):
        for copy in copies:
            copy.start()

    def come(copies):
        for copy in copies:
            copy.wait_recv()

    def leave(copies):
        for copy in copies:
            copy.wait_send()

    reach = jnp.minimum(line, lines - 1 - line)
    far = jnp.where(line < lines - 1 - line, 1, -1)

    def origin(n):
        return line + jnp.where(n <= 2 * reach, (2 * (n % 2) - 1) * ((n + 1) // 2), far * (n - reach))

    def upward(l):
        return (l <= line) & above

    def downward(l):
        return (l >= line) & below

    def arrive(n, own=False):
        l = origin(n)
        for c in range(2):
            if not own:
                along(c, l, 0).wait_recv()
            pl.when(upward(l))(along(c, l, 0).start)
            pl.when(downward(l))(along(c, l, 1).start)
            go(hop(c, l) + leap(c, l, 0))

    def meet(n):
        l = origin(n)
        for c in range(2):
            for k, copy in enumerate(hop(c, l), 1):
                copy.wait_recv()
                go(leap(c, l, k))
            cross(c, l, spot if c else odd).start()

    def add(l, p):
        terms = []
        for o in range(2):
            for s in range(half):
                pack = front[l, o, p, s]
                body, head, foot = pack[:split], pack[split : split + 16, :local], pack[split + 16 :, :local]
                right = jnp.concatenate([head, head, head, foot], axis=0)
                tile = jnp.exp(dot(left[...], right, ((1,), (0,)), None)).astype(jnp.bfloat16)
                test = jnp.concatenate([body, back[l, s, p, o]], axis=0)
                terms.append(dot(tile, test, ((1,), (0,)), None))
        while len(terms) > 1:
            terms = [a + b for a, b in zip(terms[::2], terms[1::2])] + terms[len(terms) // 2 * 2 :]
        sample[...] += terms[0]

    def close(n):
        l = origin(n)
        come(leaps(0, l))
        cross(0, l, 1 - odd).start()
        come(leaps(1, l))
        for k in range(1, half):
            cross(1, l, (spot + k) % half).start()

    def near(n):
        add(origin(n), parity)

    def last(n):
        l = origin(n)
        come([cross(0, l, j) for j in range(2)] + [cross(1, l, j) for j in range(half)])
        add(l, 1 - parity)

    def advance(n):
        arrive(n + 1)
        meet(n)

    arrive(0, True)
    each(0, lines - 1, advance)
    meet(lines - 1)
    close(0)

    def finish_line(n):
        close(n)
        near(n - 1)
        last(n - 1)

    each(1, lines, finish_line)
    near(lines - 1)
    last(lines - 1)
    def settle(l):
        for c in range(2):
            pl.when(upward(l))(along(c, l, 0).wait_send)
            pl.when(downward(l))(along(c, l, 1).wait_send)
            leave(hop(c, l) + leaps(c, l))
        leave([cross(0, l, j) for j in range(2)] + [cross(1, l, j) for j in range(half)])

    each(0, lines, settle)

    count = rows * half
    partner = col + 1 - 2 * parity
    total = sample[...]
    index = row * half + spot

    def place(i):
        return i // half, 2 * (i % half) + parity

    square[...] = dot(total.T, total, ((1,), (0,))).reshape(square.shape)
    trade = remote(square.at[1 - parity], mate, s_mate.at[0], r_mate.at[0], row, partner)
    trade.start()
    trade.wait()
    mine[...] = square[parity] + mate[...]

    def scatter(k):
        there = (index + k) % count
        r, c = place(there)
        return remote(mine.at[there], piece.at[k], s_piece.at[k], r_piece.at[k], r, c)

    each(1, count, lambda k: scatter(k).start())
    each(1, count, lambda k: scatter(k).wait())
    piece[0] = mine[index]
    done[...] = jnp.sum(piece[...], axis=0)
    gram[parity, index] = done[...]

    def collect(k):
        r, c = place((index + k) % count)
        return remote(done, gram.at[parity, index], s_done.at[k], r_done.at[k], r, c)

    def pass_on(k):
        there = (index + count - k) % count
        return remote(gram.at[parity, there], gram.at[parity, there], s_over.at[k], r_over.at[k], row, partner)

    def relay(k):
        collect(k).wait_recv()
        pass_on(k).start()

    own = remote(done, gram.at[parity, index], s_over.at[0], r_over.at[0], row, partner)
    each(1, count, lambda k: collect(k).start())
    own.start()
    each(1, count, relay)
    own.wait()
    each(1, count, lambda k: pass_on(k).wait())
    each(1, count, lambda k: collect(k).wait_send())


def sketch_gram(points, tests, rank, boundary, scales, rows, cols):
    local, ranks = tests.shape
    lines, half, count = rows // 2, cols // 2, rows * cols // 2
    lanes = 3 * (8 * ((points.shape[0] + 7) // 8)) + 8
    split = (local - lanes) // 32 * 16
    share = ranks // 2 // count
    f32 = jnp.float32
    dma = pltpu.SemaphoreType.DMA
    wide = max(2, half)
    sample, gram = pl.pallas_call(
        functools.partial(sample_kernel, rows, cols),
        out_shape=(
            jax.ShapeDtypeStruct((local, ranks), f32),
            jax.ShapeDtypeStruct((2, count, share, ranks), f32),
        ),
        in_specs=[VMEM, VMEM, VMEM, SMEM, SMEM],
        out_specs=(VMEM, VMEM),
        scratch_shapes=[
            pltpu.VMEM((lines, 2, 2, half, split + lanes, ranks), tests.dtype),
            pltpu.VMEM((lines, half, 2, 2, local - split, ranks), tests.dtype),
            pltpu.VMEM((local, 2 * lanes), tests.dtype),
            pltpu.VMEM((2, count, share, ranks), f32),
            pltpu.VMEM((count, share, ranks), f32),
            pltpu.VMEM((count, share, ranks), f32),
            pltpu.VMEM((count, share, ranks), f32),
            pltpu.VMEM((share, ranks), f32),
            dma((2, 2, lines)), dma((2, lines)),
            dma((2, lines, wide)), dma((2, lines, wide)),
            dma((2, lines, wide, wide)), dma((2, lines, wide, wide)),
            dma((2, lines, wide)), dma((2, lines, wide)),
            dma((1,)), dma((1,)), dma((count,)), dma((count,)), dma((count,)), dma((count,)), dma((count,)), dma((count,)),
        ],
        compiler_params=pltpu.CompilerParams(collective_id=0, has_side_effects=True),
        name="sketch_gram",
    )(points, tests, rank[None], boundary, scales)
    return sample, gram.reshape(ranks, ranks)


def tree(parts):
    while len(parts) > 1:
        parts = [p + q for p, q in zip(parts[::2], parts[1::2])] + parts[len(parts) // 2 * 2 :]
    return parts[0]


def sixfold(a, b):
    ah, am, al = thirds(a)
    bh, bm, bl = thirds(b)
    return jnp.concatenate([ah, ah, am, ah, al, am], axis=0), jnp.concatenate([bh, bm, bh, bl, bh, bm], axis=0)


def factor_block(a, zero):
    size, wide, width = a.shape[0], 8, 32
    shape = (wide, size)
    lane = lax.broadcasted_iota(jnp.int32, shape, 1)
    line = lax.broadcasted_iota(jnp.int32, shape, 0)

    def spread(x):
        return jnp.broadcast_to(x, shape)

    def column(x, at):
        return jnp.take_along_axis(x, zero + at, axis=1)

    rest = a
    upper, inverse = [], []
    for begin in range(0, size, width):
        end = begin + width
        blocks = [rest[i : i + wide] for i in range(0, width, wide)]
        us, ms = [], []
        marks = [column(blocks[0], begin + u) for u in range(wide)]
        for at in range(begin, end, wide):
            inside = (lane >= at) & (lane < at + wide)
            x = blocks.pop(0)
            z = jnp.where(inside, jnp.where(lane - at == line, 1.0, 0.0), x)
            y = z
            old = [[column(block, at + t) for t in range(wide)] for block in blocks]
            ahead = [column(x, at + wide + u) for u in range(wide)] if blocks else []
            fresh = [column(blocks[0], at + wide + u) for u in range(wide)] if blocks else []
            over, root = jnp.zeros(shape, jnp.float32), jnp.zeros(shape, jnp.float32)
            for s in range(wide):
                pivot = spread(marks[s][s : s + 1])
                inv = 1.0 / pivot
                over = jnp.where(line == s, inv, over)
                root = jnp.where(line == s, pivot, root)
                ratio = marks[s] * inv
                low = jnp.where(line > s, ratio, 0.0)
                both = jnp.where(line == s, 0.0, ratio)
                for u in range(s + 1, wide):
                    marks[u] = marks[u] - both * spread(marks[u][s : s + 1])
                ahead = [c - both * spread(c[s : s + 1]) for c in ahead]
                if s + 1 < wide:
                    x = x - low * spread(x[s : s + 1])
                    y = y - low * spread(y[s : s + 1])
                z = z - both * spread(z[s : s + 1])
            ahead = [c * over for c in ahead]
            marks = [
                f - tree([old[0][t] * spread(c[t : t + 1]) for t in range(wide)]) for f, c in zip(fresh, ahead)
            ]
            z = z * over
            rows = [spread(z[t : t + 1]) for t in range(wide)]
            blocks = [
                jnp.where(inside, 0.0, block) - tree([c * r for c, r in zip(columns, rows)])
                for block, columns in zip(blocks, old)
            ]
            root = lax.rsqrt(root)
            us.append(jnp.where(lane >= at + line, x * root, 0.0))
            ms.append(jnp.where(lane <= at + line, y * root, 0.0))
        u, m = jnp.concatenate(us, axis=0), jnp.concatenate(ms, axis=0)
        upper.append(u)
        inverse.append(m)
        if end < size:
            left, right = sixfold(u, jnp.where(lax.broadcasted_iota(jnp.int32, u.shape, 1) >= end, u, m))
            change = dot(left.T[end:].astype(jnp.bfloat16), right.astype(jnp.bfloat16), ((1,), (0,)), None)
            spot = lax.broadcasted_iota(jnp.int32, change.shape, 1)
            rest = jnp.where((spot >= begin) & (spot < end), 0.0, rest[width:]) - change
    return jnp.concatenate(upper, axis=0), jnp.concatenate(inverse, axis=0)


def finish_kernel(scale, gram, sample, basis, factor, up, low):
    ranks = gram.shape[0]
    half = ranks // 2
    mean = gram[...] * scale
    same = lax.broadcasted_iota(jnp.int32, (ranks, ranks), 0) == lax.broadcasted_iota(jnp.int32, (ranks, ranks), 1)
    trace = jnp.sum(jnp.sum(jnp.where(same, mean, 0.0), axis=1, keepdims=True), axis=0, keepdims=True)
    factor[...] = jnp.where(same, mean + (0.1 / ranks) * trace, mean)
    cross = factor[:half, half:]
    zero = (factor[:8, :half] * 0.0).astype(jnp.int32)

    def one(index):
        start = pl.multiple_of(index * half, half)
        block = factor[pl.ds(start, half), pl.ds(start, half)]
        u, m = factor_block(block, zero)
        up[index] = u
        low[index] = m

        @pl.when(index == 0)
        def _():
            lift = dot(m, cross, ((1,), (0,)))
            up[2] = lift
            factor[half:, half:] = factor[half:, half:] - dot(lift.T, lift, ((1,), (0,)))

    each(0, 2, one)
    lift = up[2]
    first = dot(sample[:, :half], low[0], ((1,), (1,)))
    second = dot(sample[:, half:] - dot(first, lift, ((1,), (0,))), low[1], ((1,), (1,)))
    basis[:, :half] = first
    basis[:, half:] = second
    factor[:half, :half] = up[0].T
    factor[:half, half:] = jnp.zeros((half, half), jnp.float32)
    factor[half:, :half] = lift.T
    factor[half:, half:] = up[1].T


def finish(gram, sample, everyone):
    ranks = gram.shape[0]
    half = ranks // 2
    return pl.pallas_call(
        functools.partial(finish_kernel, 1.0 / everyone),
        out_shape=(
            jax.ShapeDtypeStruct(sample.shape, jnp.float32),
            jax.ShapeDtypeStruct(gram.shape, jnp.float32),
        ),
        in_specs=[VMEM, VMEM],
        out_specs=(VMEM, VMEM),
        scratch_shapes=[pltpu.VMEM((3, half, half), jnp.float32), pltpu.VMEM((2, half, half), jnp.float32)],
        name="finish",
    )(gram, sample)


def body(rows, cols, points, sketch, rank, boundary, scales):
    sample, gram = sketch_gram(points, sketch, rank, boundary, scales, rows, cols)
    return finish(gram, sample, rows * cols * points.shape[1])


def solution(mesh):
    placed = (P(None, ("row", "col")), P(("row", "col"), None), P(("row", "col")), P(), P())
    return jax.shard_map(
        functools.partial(body, mesh.shape["row"], mesh.shape["col"]),
        mesh=mesh,
        in_specs=placed,
        out_specs=(P(("row", "col"), None), P()),
        check_vma=False,
    )
```

```python
import functools

import jax
import jax.numpy as jnp
from jax import lax
from jax.experimental import pallas as pl
from jax.experimental.pallas import tpu as pltpu
from jax.sharding import PartitionSpec as P

HIGHEST = lax.Precision.HIGHEST
FAR = 4992.0
VMEM = pl.BlockSpec(memory_space=pltpu.VMEM)
SMEM = pl.BlockSpec(memory_space=pltpu.SMEM)
HBM = pl.BlockSpec(memory_space=pltpu.HBM)


def dot(a, b, dims, precision=HIGHEST):
    return lax.dot_general(
        a, b, (dims, ((), ())), precision=precision, preferred_element_type=jnp.float32
    )


def remote(src, dst, send, recv, row, col):
    return pltpu.make_async_remote_copy(
        src_ref=src,
        dst_ref=dst,
        send_sem=send,
        recv_sem=recv,
        device_id=(row, col),
        device_id_type=pl.DeviceIdType.MESH,
    )


def each(start, stop, step):
    def run(index, carry):
        step(index)
        return carry

    lax.fori_loop(start, stop, run, 0)


def thirds(x):
    high = x.astype(jnp.bfloat16).astype(jnp.float32)
    mid = (x - high).astype(jnp.bfloat16).astype(jnp.float32)
    return high, mid, (x - high - mid).astype(jnp.bfloat16).astype(jnp.float32)


def sample_kernel(
    rows, cols, points_hbm, tests, rank_hbm, boundary, scales_hbm, sample, gram, front, back, left,
    points, rank, scales, s_in, square, mate, mine, piece, done,
    s_z, r_z, s_a, r_a, s_b, r_b, s_c, r_c,
    s_mate, r_mate, s_piece, r_piece, s_done, r_done, s_over, r_over,
):
    row, col = lax.axis_index("row"), lax.axis_index("col")
    lines, half = rows // 2, cols // 2
    line, odd = row // 2, row % 2
    spot, parity = col // 2, col % 2
    local = tests.shape[0]
    split = local - back.shape[-2]
    dims = points.shape[0]
    mesh = pl.DeviceIdType.MESH
    above, below = line < lines - 1, line > 0

    def there(l, o, s, p):
        return 2 * l + o, 2 * s + p

    barrier = pltpu.get_barrier_semaphore()

    def greet(l, o, s, p):
        pl.semaphore_signal(barrier, 1, device_id=there(l, o, s, p), device_id_type=mesh)

    @pl.when(above)
    def _():
        greet(line + 1, odd, spot, parity)

    @pl.when(below)
    def _():
        greet(line - 1, odd, spot, parity)

    for k in range(1, half):
        greet(line, odd, (spot + k) % half, parity)
    greet(line, 1 - odd, spot, parity)
    greet(line, odd, spot, 1 - parity)

    loads = [
        pltpu.make_async_copy(src, dst, s_in.at[i])
        for i, (src, dst) in enumerate([
            (scales_hbm, scales),
            (points_hbm, points),
            (rank_hbm, rank),
            (tests.at[:split], front.at[line, odd, parity, spot, :split]),
            (tests.at[split:], back.at[line, spot, parity, odd]),
        ])
    ]
    for load in loads:
        load.start()
    for load in loads[:3]:
        load.wait()
    index = lax.broadcasted_iota(jnp.int32, points.shape, 0)
    scale = jnp.ones(points.shape, jnp.float32)
    for i in range(dims):
        scale = jnp.where(index == i, scales[i], scale)
    scaled = points[...] / scale
    side = jnp.where(rank[...] >= boundary[0], 1.0, 0.0)
    gap = jnp.zeros((-dims % 8, local), jnp.float32)
    high, mid, low = [jnp.concatenate([part, gap], axis=0) if dims % 8 else part for part in thirds(scaled)]
    norms = list(thirds(-0.5 * jnp.sum(scaled * scaled, axis=0, keepdims=True)))
    ones = [jnp.ones_like(side)] * 3
    info = jnp.concatenate([high, mid, low, side, 1.0 - side] + norms + ones, axis=0)
    wide = jnp.zeros((info.shape[0], tests.shape[1] - local), jnp.float32)
    front[line, odd, parity, spot, split:] = jnp.concatenate([info, wide], axis=1).astype(jnp.bfloat16)
    left[...] = jnp.concatenate(
        [high, high, mid, mid, low, jnp.zeros_like(low), high, -FAR * side, -FAR * (1.0 - side)] + ones + norms, axis=0
    ).T.astype(jnp.bfloat16)
    sample[...] = jnp.zeros_like(sample)
    for load in loads[3:]:
        load.wait()
    pl.semaphore_wait(barrier, half + 1 + above.astype(jnp.int32) + below.astype(jnp.int32))

    def part(c, l):
        return back.at[l, spot, parity, odd] if c else front.at[l, odd, parity, spot]

    def along(c, l, down):
        return remote(part(c, l), part(c, l), s_z.at[c, down, l], r_z.at[c, l], *there(line + 1 - 2 * down, odd, spot, parity))

    def to_mate(ref, send, recv):
        return remote(ref, ref, send, recv, *there(line, 1 - odd, spot, parity))

    def to_spot(ref, k, send, recv):
        return remote(ref, ref, send, recv, *there(line, odd, (spot + k) % half, parity))

    def hop(c, l):
        if c:
            return [to_mate(part(1, l), s_a.at[1, l, 0], r_a.at[1, l, 0])]
        return [to_spot(part(0, l), k, s_a.at[0, l, k], r_a.at[0, l, k]) for k in range(1, half)]

    def leap(c, l, k):
        if c:
            return [
                to_spot(back.at[l, spot, parity, (odd + k) % 2], j, s_b.at[1, l, k, j], r_b.at[1, l, k, j])
                for j in range(1, half)
            ]
        return [to_mate(front.at[l, odd, parity, (spot + half - k) % half], s_b.at[0, l, k, 0], r_b.at[0, l, k, 0])]

    def leaps(c, l):
        return [copy for k in range(2 if c else half) for copy in leap(c, l, k)]

    def cross(c, l, j):
        ref = back.at[l, j, parity] if c else front.at[l, j, parity]
        return remote(ref, ref, s_c.at[c, l, j], r_c.at[c, l, j], *there(line, odd, spot, 1 - parity))

    def go(copies):
        for copy in copies:
            copy.start()

    def come(copies):
        for copy in copies:
            copy.wait_recv()

    def leave(copies):
        for copy in copies:
            copy.wait_send()

    reach = jnp.minimum(line, lines - 1 - line)
    far = jnp.where(line < lines - 1 - line, 1, -1)

    def origin(n):
        return line + jnp.where(n <= 2 * reach, (2 * (n % 2) - 1) * ((n + 1) // 2), far * (n - reach))

    def upward(l):
        return (l <= line) & above

    def downward(l):
        return (l >= line) & below

    def arrive(n, own=False):
        l = origin(n)
        for c in range(2):
            if not own:
                along(c, l, 0).wait_recv()
            pl.when(upward(l))(along(c, l, 0).start)
            pl.when(downward(l))(along(c, l, 1).start)
            go(hop(c, l) + leap(c, l, 0))

    def meet(n):
        l = origin(n)
        for c in range(2):
            for k, copy in enumerate(hop(c, l), 1):
                copy.wait_recv()
                go(leap(c, l, k))
            cross(c, l, spot if c else odd).start()

    def add(l, p):
        terms = []
        for o in range(2):
            for s in range(half):
                pack = front[l, o, p, s]
                body, head, foot = pack[:split], pack[split : split + 16, :local], pack[split + 16 :, :local]
                right = jnp.concatenate([head, head, head, foot], axis=0)
                tile = jnp.exp(dot(left[...], right, ((1,), (0,)), None)).astype(jnp.bfloat16)
                test = jnp.concatenate([body, back[l, s, p, o]], axis=0)
                terms.append(dot(tile, test, ((1,), (0,)), None))
        while len(terms) > 1:
            terms = [a + b for a, b in zip(terms[::2], terms[1::2])] + terms[len(terms) // 2 * 2 :]
        sample[...] += terms[0]

    def close(n):
        l = origin(n)
        come(leaps(0, l))
        cross(0, l, 1 - odd).start()
        come(leaps(1, l))
        for k in range(1, half):
            cross(1, l, (spot + k) % half).start()

    def near(n):
        add(origin(n), parity)

    def last(n):
        l = origin(n)
        come([cross(0, l, j) for j in range(2)] + [cross(1, l, j) for j in range(half)])
        add(l, 1 - parity)

    def advance(n):
        arrive(n + 1)
        meet(n)

    arrive(0, True)
    each(0, lines - 1, advance)
    meet(lines - 1)
    close(0)

    def finish_line(n):
        close(n)
        near(n - 1)
        last(n - 1)

    each(1, lines, finish_line)
    near(lines - 1)
    last(lines - 1)
    def settle(l):
        for c in range(2):
            pl.when(upward(l))(along(c, l, 0).wait_send)
            pl.when(downward(l))(along(c, l, 1).wait_send)
            leave(hop(c, l) + leaps(c, l))
        leave([cross(0, l, j) for j in range(2)] + [cross(1, l, j) for j in range(half)])

    each(0, lines, settle)

    count = rows * half
    partner = col + 1 - 2 * parity
    total = sample[...]
    index = row * half + spot

    def place(i):
        return i // half, 2 * (i % half) + parity

    square[...] = dot(total.T, total, ((1,), (0,))).reshape(square.shape)
    trade = remote(square.at[1 - parity], mate, s_mate.at[0], r_mate.at[0], row, partner)
    trade.start()
    trade.wait()
    mine[...] = square[parity] + mate[...]

    def scatter(k):
        there = (index + k) % count
        r, c = place(there)
        return remote(mine.at[there], piece.at[k], s_piece.at[k], r_piece.at[k], r, c)

    each(1, count, lambda k: scatter(k).start())
    each(1, count, lambda k: scatter(k).wait())
    piece[0] = mine[index]
    done[...] = jnp.sum(piece[...], axis=0)
    gram[parity, index] = done[...]

    def collect(k):
        r, c = place((index + k) % count)
        return remote(done, gram.at[parity, index], s_done.at[k], r_done.at[k], r, c)

    def pass_on(k):
        there = (index + count - k) % count
        return remote(gram.at[parity, there], gram.at[parity, there], s_over.at[k], r_over.at[k], row, partner)

    def relay(k):
        collect(k).wait_recv()
        pass_on(k).start()

    own = remote(done, gram.at[parity, index], s_over.at[0], r_over.at[0], row, partner)
    each(1, count, lambda k: collect(k).start())
    own.start()
    each(1, count, relay)
    own.wait()
    each(1, count, lambda k: pass_on(k).wait())
    each(1, count, lambda k: collect(k).wait_send())


def far(x):
    return pltpu.with_memory_space_constraint(x, pltpu.HBM)


def sketch_gram(points, tests, rank, boundary, scales, rows, cols):
    local, ranks = tests.shape
    lines, half, count = rows // 2, cols // 2, rows * cols // 2
    lanes = 3 * (8 * ((points.shape[0] + 7) // 8)) + 8
    split = (local - lanes) // 32 * 16
    share = ranks // 2 // count
    f32 = jnp.float32
    dma = pltpu.SemaphoreType.DMA
    wide = max(2, half)
    sample, gram = pl.pallas_call(
        functools.partial(sample_kernel, rows, cols),
        out_shape=(
            jax.ShapeDtypeStruct((local, ranks), f32),
            jax.ShapeDtypeStruct((2, count, share, ranks), f32),
        ),
        in_specs=[HBM, HBM, HBM, SMEM, HBM],
        out_specs=(VMEM, VMEM),
        scratch_shapes=[
            pltpu.VMEM((lines, 2, 2, half, split + lanes, ranks), tests.dtype),
            pltpu.VMEM((lines, half, 2, 2, local - split, ranks), tests.dtype),
            pltpu.VMEM((local, 2 * lanes), tests.dtype),
            pltpu.VMEM(points.shape, f32), pltpu.VMEM((1, local), rank.dtype), pltpu.SMEM(scales.shape, f32), dma((5,)),
            pltpu.VMEM((2, count, share, ranks), f32),
            pltpu.VMEM((count, share, ranks), f32),
            pltpu.VMEM((count, share, ranks), f32),
            pltpu.VMEM((count, share, ranks), f32),
            pltpu.VMEM((share, ranks), f32),
            dma((2, 2, lines)), dma((2, lines)),
            dma((2, lines, wide)), dma((2, lines, wide)),
            dma((2, lines, wide, wide)), dma((2, lines, wide, wide)),
            dma((2, lines, wide)), dma((2, lines, wide)),
            dma((1,)), dma((1,)), dma((count,)), dma((count,)), dma((count,)), dma((count,)), dma((count,)), dma((count,)),
        ],
        compiler_params=pltpu.CompilerParams(
            collective_id=0,
            has_side_effects=True,
            vmem_limit_bytes=2 * rows * cols * (local + lanes) * ranks + 8 * 2**20,
        ),
        name="sketch_gram",
    )(far(points), far(tests), far(rank[None]), boundary, far(scales))
    return sample, gram.reshape(ranks, ranks)


def tree(parts):
    while len(parts) > 1:
        parts = [p + q for p, q in zip(parts[::2], parts[1::2])] + parts[len(parts) // 2 * 2 :]
    return parts[0]


def sixfold(a, b):
    ah, am, al = thirds(a)
    bh, bm, bl = thirds(b)
    return jnp.concatenate([ah, ah, am, ah, al, am], axis=0), jnp.concatenate([bh, bm, bh, bl, bh, bm], axis=0)


def factor_block(a, zero):
    size, wide, width = a.shape[0], 8, 32
    shape = (wide, size)
    lane = lax.broadcasted_iota(jnp.int32, shape, 1)
    line = lax.broadcasted_iota(jnp.int32, shape, 0)

    def spread(x):
        return jnp.broadcast_to(x, shape)

    def column(x, at):
        return jnp.take_along_axis(x, zero + at, axis=1, mode="promise_in_bounds")

    rest = a
    upper, inverse = [], []
    for begin in range(0, size, width):
        end = begin + width
        blocks = [rest[i : i + wide] for i in range(0, width, wide)]
        us, ms = [], []
        marks = [column(blocks[0], begin + u) for u in range(wide)]
        for at in range(begin, end, wide):
            inside = (lane >= at) & (lane < at + wide)
            x = blocks.pop(0)
            z = jnp.where(inside, jnp.where(lane - at == line, 1.0, 0.0), x)
            y = z
            old = [[column(block, at + t) for t in range(wide)] for block in blocks]
            ahead = [column(x, at + wide + u) for u in range(wide)] if blocks else []
            fresh = [column(blocks[0], at + wide + u) for u in range(wide)] if blocks else []
            over, root = jnp.zeros(shape, jnp.float32), jnp.zeros(shape, jnp.float32)
            for s in range(wide):
                pivot = spread(marks[s][s : s + 1])
                inv = 1.0 / pivot
                over = jnp.where(line == s, inv, over)
                root = jnp.where(line == s, pivot, root)
                ratio = marks[s] * inv
                low = jnp.where(line > s, ratio, 0.0)
                both = jnp.where(line == s, 0.0, ratio)
                for u in range(s + 1, wide):
                    marks[u] = marks[u] - both * spread(marks[u][s : s + 1])
                ahead = [c - both * spread(c[s : s + 1]) for c in ahead]
                if s + 1 < wide:
                    x = x - low * spread(x[s : s + 1])
                    y = y - low * spread(y[s : s + 1])
                z = z - both * spread(z[s : s + 1])
            ahead = [c * over for c in ahead]
            marks = [
                f - tree([old[0][t] * spread(c[t : t + 1]) for t in range(wide)]) for f, c in zip(fresh, ahead)
            ]
            z = z * over
            rows = [spread(z[t : t + 1]) for t in range(wide)]
            blocks = [
                jnp.where(inside, 0.0, block) - tree([c * r for c, r in zip(columns, rows)])
                for block, columns in zip(blocks, old)
            ]
            root = lax.rsqrt(root)
            us.append(jnp.where(lane >= at + line, x * root, 0.0))
            ms.append(jnp.where(lane <= at + line, y * root, 0.0))
        u, m = jnp.concatenate(us, axis=0), jnp.concatenate(ms, axis=0)
        upper.append(u)
        inverse.append(m)
        if end < size:
            left, right = sixfold(u, jnp.where(lax.broadcasted_iota(jnp.int32, u.shape, 1) >= end, u, m))
            change = dot(left.T[end:].astype(jnp.bfloat16), right.astype(jnp.bfloat16), ((1,), (0,)), None)
            spot = lax.broadcasted_iota(jnp.int32, change.shape, 1)
            rest = jnp.where((spot >= begin) & (spot < end), 0.0, rest[width:]) - change
    return jnp.concatenate(upper, axis=0), jnp.concatenate(inverse, axis=0)


def product(a, b, dims):
    (i,), (j,) = dims
    ah, am, al = [part.astype(jnp.bfloat16) for part in thirds(a)]
    bh, bm, bl = [part.astype(jnp.bfloat16) for part in thirds(b)]
    return dot(jnp.concatenate([ah, ah, am, ah, al, am], axis=i), jnp.concatenate([bh, bm, bh, bl, bh, bm], axis=j), dims, None)


def finish_kernel(scale, gram, sample, basis, factor):
    ranks = gram.shape[0]
    half = ranks // 2
    mean = gram[...] * scale
    same = lax.broadcasted_iota(jnp.int32, (ranks, ranks), 0) == lax.broadcasted_iota(jnp.int32, (ranks, ranks), 1)
    trace = jnp.sum(jnp.sum(jnp.where(same, mean, 0.0), axis=0, keepdims=True), axis=1, keepdims=True)
    shifted = jnp.where(same, mean + (0.1 / ranks) * trace, mean)
    zero = (mean[:8, :half] * 0.0).astype(jnp.int32)
    up, low = factor_block(shifted[:half, :half], zero)
    lift = product(low, shifted[:half, half:], ((1,), (0,)))
    up2, low2 = factor_block(shifted[half:, half:] - product(lift.T, lift, ((1,), (0,))), zero)
    first = product(sample[:, :half], low, ((1,), (1,)))
    rest = sample[:, half:] - product(first, lift, ((1,), (0,)))
    basis[:, :half] = first
    basis[:, half:] = product(rest, low2, ((1,), (1,)))
    factor[:half, :half] = up.T
    factor[:half, half:] = jnp.zeros((half, half), jnp.float32)
    factor[half:, :half] = lift.T
    factor[half:, half:] = up2.T


def finish(gram, sample, everyone):
    return pl.pallas_call(
        functools.partial(finish_kernel, 1.0 / everyone),
        out_shape=(
            jax.ShapeDtypeStruct(sample.shape, jnp.float32),
            jax.ShapeDtypeStruct(gram.shape, jnp.float32),
        ),
        in_specs=[VMEM, VMEM],
        out_specs=(VMEM, VMEM),
        compiler_params=pltpu.CompilerParams(vmem_limit_bytes=8 * 2**20),
        name="finish",
    )(gram, sample)


def body(rows, cols, points, sketch, rank, boundary, scales):
    sample, gram = sketch_gram(points, sketch, rank, boundary, scales, rows, cols)
    return finish(gram, sample, rows * cols * points.shape[1])


def solution(mesh):
    placed = (P(None, ("row", "col")), P(("row", "col"), None), P(("row", "col")), P(), P())
    return jax.shard_map(
        functools.partial(body, mesh.shape["row"], mesh.shape["col"]),
        mesh=mesh,
        in_specs=placed,
        out_specs=(P(("row", "col"), None), P()),
        check_vma=False,
    )
```

```python
import functools

import jax
import jax.numpy as jnp
from jax import lax
from jax.experimental import pallas as pl
from jax.experimental.pallas import tpu as pltpu
from jax.sharding import PartitionSpec as P

HIGHEST = lax.Precision.HIGHEST
FAR = 4992.0
VMEM = pl.BlockSpec(memory_space=pltpu.VMEM)
SMEM = pl.BlockSpec(memory_space=pltpu.SMEM)
HBM = pl.BlockSpec(memory_space=pltpu.HBM)


def dot(a, b, dims, precision=HIGHEST):
    return lax.dot_general(
        a, b, (dims, ((), ())), precision=precision, preferred_element_type=jnp.float32
    )


def remote(src, dst, send, recv, row, col):
    return pltpu.make_async_remote_copy(
        src_ref=src,
        dst_ref=dst,
        send_sem=send,
        recv_sem=recv,
        device_id=(row, col),
        device_id_type=pl.DeviceIdType.MESH,
    )


def each(start, stop, step):
    def run(index, carry):
        step(index)
        return carry

    lax.fori_loop(start, stop, run, 0)


def thirds(x):
    high = x.astype(jnp.bfloat16).astype(jnp.float32)
    mid = (x - high).astype(jnp.bfloat16).astype(jnp.float32)
    return high, mid, (x - high - mid).astype(jnp.bfloat16).astype(jnp.float32)


def sample_kernel(
    rows, cols, points_hbm, tests, rank_hbm, boundary, scales_hbm, sample, gram, front, back, left,
    points, rank, scales, s_in, square, mate, mine, piece, done,
    s_z, r_z, s_a, r_a, s_b, r_b, s_c, r_c,
    s_mate, r_mate, s_piece, r_piece, s_done, r_done, s_over, r_over,
):
    row, col = lax.axis_index("row"), lax.axis_index("col")
    lines, half = rows // 2, cols // 2
    line, odd = row // 2, row % 2
    spot, parity = col // 2, col % 2
    local = tests.shape[0]
    split = local - back.shape[-2]
    dims = points.shape[0]
    mesh = pl.DeviceIdType.MESH
    above, below = line < lines - 1, line > 0

    def there(l, o, s, p):
        return 2 * l + o, 2 * s + p

    barrier = pltpu.get_barrier_semaphore()

    def greet(l, o, s, p):
        pl.semaphore_signal(barrier, 1, device_id=there(l, o, s, p), device_id_type=mesh)

    @pl.when(above)
    def _():
        greet(line + 1, odd, spot, parity)

    @pl.when(below)
    def _():
        greet(line - 1, odd, spot, parity)

    for k in range(1, half):
        greet(line, odd, (spot + k) % half, parity)
    greet(line, 1 - odd, spot, parity)
    greet(line, odd, spot, 1 - parity)

    loads = [
        pltpu.make_async_copy(src, dst, s_in.at[i])
        for i, (src, dst) in enumerate([
            (scales_hbm, scales),
            (points_hbm, points),
            (rank_hbm, rank),
            (tests.at[:split], front.at[line, odd, parity, spot, :split]),
            (tests.at[split:], back.at[line, spot, parity, odd]),
        ])
    ]
    for load in loads:
        load.start()
    for load in loads[:3]:
        load.wait()
    index = lax.broadcasted_iota(jnp.int32, points.shape, 0)
    scale = jnp.ones(points.shape, jnp.float32)
    for i in range(dims):
        scale = jnp.where(index == i, scales[i], scale)
    scaled = points[...] / scale
    side = jnp.where(rank[...] >= boundary[0], 1.0, 0.0)
    gap = jnp.zeros((-dims % 8, local), jnp.float32)
    high, mid, low = [jnp.concatenate([part, gap], axis=0) if dims % 8 else part for part in thirds(scaled)]
    norms = list(thirds(-0.5 * jnp.sum(scaled * scaled, axis=0, keepdims=True)))
    ones = [jnp.ones_like(side)] * 3
    info = jnp.concatenate([high, mid, low, side, 1.0 - side] + norms + ones, axis=0)
    wide = jnp.zeros((info.shape[0], tests.shape[1] - local), jnp.float32)
    front[line, odd, parity, spot, split:] = jnp.concatenate([info, wide], axis=1).astype(jnp.bfloat16)
    left[...] = jnp.concatenate(
        [high, high, mid, mid, low, jnp.zeros_like(low), high, -FAR * side, -FAR * (1.0 - side)] + ones + norms, axis=0
    ).T.astype(jnp.bfloat16)
    sample[...] = jnp.zeros_like(sample)
    for load in loads[3:]:
        load.wait()
    pl.semaphore_wait(barrier, half + 1 + above.astype(jnp.int32) + below.astype(jnp.int32))

    def part(c, l):
        return back.at[l, spot, parity, odd] if c else front.at[l, odd, parity, spot]

    def along(c, l, down):
        return remote(part(c, l), part(c, l), s_z.at[c, down, l], r_z.at[c, l], *there(line + 1 - 2 * down, odd, spot, parity))

    def to_mate(ref, send, recv):
        return remote(ref, ref, send, recv, *there(line, 1 - odd, spot, parity))

    def to_spot(ref, k, send, recv):
        return remote(ref, ref, send, recv, *there(line, odd, (spot + k) % half, parity))

    def hop(c, l):
        if c:
            return [to_mate(part(1, l), s_a.at[1, l, 0], r_a.at[1, l, 0])]
        return [to_spot(part(0, l), k, s_a.at[0, l, k], r_a.at[0, l, k]) for k in range(1, half)]

    def leap(c, l, k):
        if c:
            return [
                to_spot(back.at[l, spot, parity, (odd + k) % 2], j, s_b.at[1, l, k, j], r_b.at[1, l, k, j])
                for j in range(1, half)
            ]
        return [to_mate(front.at[l, odd, parity, (spot + half - k) % half], s_b.at[0, l, k, 0], r_b.at[0, l, k, 0])]

    def leaps(c, l):
        return [copy for k in range(2 if c else half) for copy in leap(c, l, k)]

    def cross(c, l, j):
        ref = back.at[l, j, parity] if c else front.at[l, j, parity]
        return remote(ref, ref, s_c.at[c, l, j], r_c.at[c, l, j], *there(line, odd, spot, 1 - parity))

    def go(copies):
        for copy in copies:
            copy.start()

    def come(copies):
        for copy in copies:
            copy.wait_recv()

    def leave(copies):
        for copy in copies:
            copy.wait_send()

    reach = jnp.minimum(line, lines - 1 - line)
    far = jnp.where(line < lines - 1 - line, 1, -1)

    def origin(n):
        return line + jnp.where(n <= 2 * reach, (2 * (n % 2) - 1) * ((n + 1) // 2), far * (n - reach))

    def upward(l):
        return (l <= line) & above

    def downward(l):
        return (l >= line) & below

    def arrive(n, own=False):
        l = origin(n)
        for c in range(2):
            if not own:
                along(c, l, 0).wait_recv()
            pl.when(upward(l))(along(c, l, 0).start)
            pl.when(downward(l))(along(c, l, 1).start)
            go(hop(c, l) + leap(c, l, 0))

    def meet(n):
        l = origin(n)
        for c in range(2):
            for k, copy in enumerate(hop(c, l), 1):
                copy.wait_recv()
                go(leap(c, l, k))
            cross(c, l, spot if c else odd).start()

    def add(l, p):
        terms = []
        for o in range(2):
            for s in range(half):
                pack = front[l, o, p, s]
                body, head, foot = pack[:split], pack[split : split + 16, :local], pack[split + 16 :, :local]
                right = jnp.concatenate([head, head, head, foot], axis=0)
                tile = jnp.exp(dot(left[...], right, ((1,), (0,)), None)).astype(jnp.bfloat16)
                test = jnp.concatenate([body, back[l, s, p, o]], axis=0)
                terms.append(dot(tile, test, ((1,), (0,)), None))
        while len(terms) > 1:
            terms = [a + b for a, b in zip(terms[::2], terms[1::2])] + terms[len(terms) // 2 * 2 :]
        sample[...] += terms[0]

    def close(n):
        l = origin(n)
        come(leaps(0, l))
        cross(0, l, 1 - odd).start()
        come(leaps(1, l))
        for k in range(1, half):
            cross(1, l, (spot + k) % half).start()

    def near(n):
        add(origin(n), parity)

    def last(n):
        l = origin(n)
        come([cross(0, l, j) for j in range(2)] + [cross(1, l, j) for j in range(half)])
        add(l, 1 - parity)

    def advance(n):
        arrive(n + 1)
        meet(n)

    arrive(0, True)
    each(0, lines - 1, advance)
    meet(lines - 1)
    close(0)

    def finish_line(n):
        close(n)
        near(n - 1)
        last(n - 1)

    each(1, lines, finish_line)
    near(lines - 1)
    last(lines - 1)
    def settle(l):
        for c in range(2):
            pl.when(upward(l))(along(c, l, 0).wait_send)
            pl.when(downward(l))(along(c, l, 1).wait_send)
            leave(hop(c, l) + leaps(c, l))
        leave([cross(0, l, j) for j in range(2)] + [cross(1, l, j) for j in range(half)])

    each(0, lines, settle)

    count = rows * half
    partner = col + 1 - 2 * parity
    total = sample[...]
    index = row * half + spot

    def place(i):
        return lax.div(i, half), 2 * lax.rem(i, half) + parity

    ranks = total.shape[1]

    def cut(ref, low):
        return ref.at[:, ranks // 2 :] if low else ref

    def cuts(ref, low):
        return ref.at[:, :, ranks // 2 :] if low else ref

    def mine_or(make, act):
        for low in range(2):
            pl.when(parity == low)(lambda low=low: act(make(low)))

    def other(make, act):
        for low in range(2):
            pl.when(parity == 1 - low)(lambda low=low: act(make(low)))

    def begin(copy):
        copy.start()

    def got(copy):
        copy.wait_recv()

    def sent(copy):
        copy.wait_send()

    def both(copy):
        copy.wait()

    square[...] = product(total, total, ((0,), (0,))).reshape(square.shape)

    def trade(low):
        return remote(cuts(square.at[low], low), cuts(mate, low), s_mate.at[0], r_mate.at[0], row, partner)

    other(trade, begin)
    mine_or(trade, got)
    mine[...] = square[parity] + mate[...]

    def scatter(k):
        there = lax.rem(index + k, count)
        r, c = place(there)
        return lambda low: remote(cut(mine.at[there], low), cut(piece.at[k], low), s_piece.at[k], r_piece.at[k], r, c)

    each(1, count, lambda k: mine_or(scatter(k), begin))
    each(1, count, lambda k: mine_or(scatter(k), both))
    piece[0] = mine[index]
    done[...] = jnp.sum(piece[...], axis=0)
    gram[parity, index] = done[...]

    def collect(k):
        r, c = place(lax.rem(index + k, count))
        return lambda low: remote(cut(done, low), cut(gram.at[parity, index], low), s_done.at[k], r_done.at[k], r, c)

    def pass_on(k):
        there = lax.rem(index + count - k, count)

        def make(low):
            ref = cut(gram.at[low, there], low)
            return remote(ref, ref, s_over.at[k], r_over.at[k], row, partner)

        return make

    def relay(k):
        mine_or(collect(k), got)
        mine_or(pass_on(k), begin)

    def own(low):
        return remote(cut(done, low), cut(gram.at[low, index], low), s_over.at[0], r_over.at[0], row, partner)

    each(1, count, lambda k: mine_or(collect(k), begin))
    mine_or(own, begin)
    each(1, count, relay)
    mine_or(own, sent)
    other(own, got)

    def last_waits(k):
        mine_or(pass_on(k), sent)
        other(pass_on(k), got)
        mine_or(collect(k), sent)

    each(1, count, last_waits)
    other(trade, sent)


def far(x):
    return pltpu.with_memory_space_constraint(x, pltpu.HBM)


def sketch_gram(points, tests, rank, boundary, scales, rows, cols):
    local, ranks = tests.shape
    lines, half, count = rows // 2, cols // 2, rows * cols // 2
    lanes = 3 * (8 * ((points.shape[0] + 7) // 8)) + 8
    split = (local - lanes) // 32 * 16
    share = ranks // 2 // count
    f32 = jnp.float32
    dma = pltpu.SemaphoreType.DMA
    wide = max(2, half)
    sample, gram = pl.pallas_call(
        functools.partial(sample_kernel, rows, cols),
        out_shape=(
            jax.ShapeDtypeStruct((local, ranks), f32),
            jax.ShapeDtypeStruct((2, count, share, ranks), f32),
        ),
        in_specs=[HBM, HBM, HBM, SMEM, HBM],
        out_specs=(VMEM, VMEM),
        scratch_shapes=[
            pltpu.VMEM((lines, 2, 2, half, split + lanes, ranks), tests.dtype),
            pltpu.VMEM((lines, half, 2, 2, local - split, ranks), tests.dtype),
            pltpu.VMEM((local, 2 * lanes), tests.dtype),
            pltpu.VMEM(points.shape, f32), pltpu.VMEM((1, local), rank.dtype), pltpu.SMEM(scales.shape, f32), dma((5,)),
            pltpu.VMEM((2, count, share, ranks), f32),
            pltpu.VMEM((count, share, ranks), f32),
            pltpu.VMEM((count, share, ranks), f32),
            pltpu.VMEM((count, share, ranks), f32),
            pltpu.VMEM((share, ranks), f32),
            dma((2, 2, lines)), dma((2, lines)),
            dma((2, lines, wide)), dma((2, lines, wide)),
            dma((2, lines, wide, wide)), dma((2, lines, wide, wide)),
            dma((2, lines, wide)), dma((2, lines, wide)),
            dma((1,)), dma((1,)), dma((count,)), dma((count,)), dma((count,)), dma((count,)), dma((count,)), dma((count,)),
        ],
        compiler_params=pltpu.CompilerParams(
            collective_id=0,
            has_side_effects=True,
            vmem_limit_bytes=2 * rows * cols * (local + lanes) * ranks + 8 * 2**20,
        ),
        name="sketch_gram",
    )(far(points), far(tests), far(rank[None]), boundary, far(scales))
    return sample, gram.reshape(ranks, ranks)


def tree(parts):
    while len(parts) > 1:
        parts = [p + q for p, q in zip(parts[::2], parts[1::2])] + parts[len(parts) // 2 * 2 :]
    return parts[0]


def sixfold(a, b):
    ah, am, al = thirds(a)
    bh, bm, bl = thirds(b)
    return jnp.concatenate([ah, ah, am, ah, al, am], axis=0), jnp.concatenate([bh, bm, bh, bl, bh, bm], axis=0)


def factor_block(a, zero):
    size, wide, width = a.shape[0], 8, 32
    shape = (wide, size)
    lane = lax.broadcasted_iota(jnp.int32, shape, 1)
    line = lax.broadcasted_iota(jnp.int32, shape, 0)

    def spread(x):
        return jnp.broadcast_to(x, shape)

    def column(x, at):
        return jnp.take_along_axis(x, zero + at, axis=1, mode="promise_in_bounds")

    rest = a
    upper, inverse = [], []
    for begin in range(0, size, width):
        end = begin + width
        blocks = [rest[i : i + wide] for i in range(0, width, wide)]
        us, ms = [], []
        marks = [column(blocks[0], begin + u) for u in range(wide)]
        for at in range(begin, end, wide):
            inside = (lane >= at) & (lane < at + wide)
            x = blocks.pop(0)
            z = jnp.where(inside, jnp.where(lane - at == line, 1.0, 0.0), x)
            y = z
            old = [[column(block, at + t) for t in range(wide)] for block in blocks]
            ahead = [column(x, at + wide + u) for u in range(wide)] if blocks else []
            fresh = [column(blocks[0], at + wide + u) for u in range(wide)] if blocks else []
            over, root = jnp.zeros(shape, jnp.float32), jnp.zeros(shape, jnp.float32)
            for s in range(wide):
                pivot = spread(marks[s][s : s + 1])
                inv = 1.0 / pivot
                over = jnp.where(line == s, inv, over)
                root = jnp.where(line == s, pivot, root)
                ratio = marks[s] * inv
                low = jnp.where(line > s, ratio, 0.0)
                both = jnp.where(line == s, 0.0, ratio)
                for u in range(s + 1, wide):
                    marks[u] = marks[u] - both * spread(marks[u][s : s + 1])
                ahead = [c - both * spread(c[s : s + 1]) for c in ahead]
                if s + 1 < wide:
                    x = x - low * spread(x[s : s + 1])
                    y = y - low * spread(y[s : s + 1])
                z = z - both * spread(z[s : s + 1])
            ahead = [c * over for c in ahead]
            marks = [
                f - tree([old[0][t] * spread(c[t : t + 1]) for t in range(wide)]) for f, c in zip(fresh, ahead)
            ]
            z = z * over
            rows = [spread(z[t : t + 1]) for t in range(wide)]
            blocks = [
                jnp.where(inside, 0.0, block) - tree([c * r for c, r in zip(columns, rows)])
                for block, columns in zip(blocks, old)
            ]
            root = lax.rsqrt(root)
            us.append(jnp.where(lane >= at + line, x * root, 0.0))
            ms.append(jnp.where(lane <= at + line, y * root, 0.0))
        u, m = jnp.concatenate(us, axis=0), jnp.concatenate(ms, axis=0)
        upper.append(u)
        inverse.append(m)
        if end < size:
            left, right = sixfold(u, jnp.where(lax.broadcasted_iota(jnp.int32, u.shape, 1) >= end, u, m))
            change = dot(left.T[end:].astype(jnp.bfloat16), right.astype(jnp.bfloat16), ((1,), (0,)), None)
            spot = lax.broadcasted_iota(jnp.int32, change.shape, 1)
            rest = jnp.where((spot >= begin) & (spot < end), 0.0, rest[width:]) - change
    return jnp.concatenate(upper, axis=0), jnp.concatenate(inverse, axis=0)


def product(a, b, dims):
    (i,), (j,) = dims
    ah, am, al = [part.astype(jnp.bfloat16) for part in thirds(a)]
    bh, bm, bl = [part.astype(jnp.bfloat16) for part in thirds(b)]
    return dot(jnp.concatenate([ah, ah, am, ah, al, am], axis=i), jnp.concatenate([bh, bm, bh, bl, bh, bm], axis=j), dims, None)


def finish_kernel(scale, gram, sample, basis, factor):
    half = gram.shape[0] // 2
    head, cross, foot = [part * scale for part in (gram[:half, :half], gram[:half, half:], gram[half:, half:])]
    same = lax.broadcasted_iota(jnp.int32, (half, half), 0) == lax.broadcasted_iota(jnp.int32, (half, half), 1)
    trace = jnp.sum(jnp.sum(jnp.where(same, head + foot, 0.0), axis=0, keepdims=True), axis=1, keepdims=True)
    shift = jnp.where(same, (0.05 / half) * trace, 0.0)
    zero = (head[:8] * 0.0).astype(jnp.int32)
    up, low = factor_block(head + shift, zero)
    lift = product(low, cross, ((1,), (0,)))
    up2, low2 = factor_block(foot + shift - product(lift.T, lift, ((1,), (0,))), zero)
    first = product(sample[:, :half], low, ((1,), (1,)))
    rest = sample[:, half:] - product(first, lift, ((1,), (0,)))
    basis[:, :half] = first
    basis[:, half:] = product(rest, low2, ((1,), (1,)))
    factor[:half, :half] = up.T
    factor[:half, half:] = jnp.zeros((half, half), jnp.float32)
    factor[half:, :half] = lift.T
    factor[half:, half:] = up2.T


def finish(gram, sample, everyone):
    return pl.pallas_call(
        functools.partial(finish_kernel, 1.0 / everyone),
        out_shape=(
            jax.ShapeDtypeStruct(sample.shape, jnp.float32),
            jax.ShapeDtypeStruct(gram.shape, jnp.float32),
        ),
        in_specs=[VMEM, VMEM],
        out_specs=(VMEM, VMEM),
        compiler_params=pltpu.CompilerParams(vmem_limit_bytes=8 * 2**20),
        name="finish",
    )(gram, sample)


def body(rows, cols, points, sketch, rank, boundary, scales):
    sample, gram = sketch_gram(points, sketch, rank, boundary, scales, rows, cols)
    return finish(gram, sample, rows * cols * points.shape[1])


def solution(mesh):
    placed = (P(None, ("row", "col")), P(("row", "col"), None), P(("row", "col")), P(), P())
    return jax.shard_map(
        functools.partial(body, mesh.shape["row"], mesh.shape["col"]),
        mesh=mesh,
        in_specs=placed,
        out_specs=(P(("row", "col"), None), P()),
        check_vma=False,
    )
```

```python
import functools

import jax
import jax.numpy as jnp
from jax import lax
from jax.experimental import pallas as pl
from jax.experimental.pallas import tpu as pltpu
from jax.sharding import PartitionSpec as P

HIGHEST = lax.Precision.HIGHEST
FAR = 4992.0
VMEM = pl.BlockSpec(memory_space=pltpu.VMEM)
SMEM = pl.BlockSpec(memory_space=pltpu.SMEM)
HBM = pl.BlockSpec(memory_space=pltpu.HBM)


def dot(a, b, dims, precision=HIGHEST):
    return lax.dot_general(
        a, b, (dims, ((), ())), precision=precision, preferred_element_type=jnp.float32
    )


def remote(src, dst, send, recv, row, col):
    return pltpu.make_async_remote_copy(
        src_ref=src,
        dst_ref=dst,
        send_sem=send,
        recv_sem=recv,
        device_id=(row, col),
        device_id_type=pl.DeviceIdType.MESH,
    )


def each(start, stop, step):
    def run(index, carry):
        step(index)
        return carry

    lax.fori_loop(start, stop, run, 0)


def thirds(x):
    high = x.astype(jnp.bfloat16).astype(jnp.float32)
    mid = (x - high).astype(jnp.bfloat16).astype(jnp.float32)
    return high, mid, (x - high - mid).astype(jnp.bfloat16).astype(jnp.float32)


def sample_kernel(
    rows, cols, points_hbm, tests, rank_hbm, boundary, scales_hbm, sample, gram, front, back, left,
    points, rank, scales, s_in, square, mate, mine, piece, done,
    s_all, r_z, r_a, r_b, r_c, s_mate, r_mate, r_piece, r_done, r_over,
):
    row, col = lax.axis_index("row"), lax.axis_index("col")
    lines, half = rows // 2, cols // 2
    line, odd = row // 2, row % 2
    spot, parity = col // 2, col % 2
    local = tests.shape[0]
    split = local - back.shape[-2]
    dims = points.shape[0]
    mesh = pl.DeviceIdType.MESH
    above, below = line < lines - 1, line > 0

    def there(l, o, s, p):
        return 2 * l + o, 2 * s + p

    barrier = pltpu.get_barrier_semaphore()

    def greet(l, o, s, p):
        pl.semaphore_signal(barrier, 1, device_id=there(l, o, s, p), device_id_type=mesh)

    @pl.when(above)
    def _():
        greet(line + 1, odd, spot, parity)

    @pl.when(below)
    def _():
        greet(line - 1, odd, spot, parity)

    for k in range(1, half):
        greet(line, odd, (spot + k) % half, parity)
    greet(line, 1 - odd, spot, parity)
    greet(line, odd, spot, 1 - parity)

    loads = [
        pltpu.make_async_copy(src, dst, s_in.at[i])
        for i, (src, dst) in enumerate([
            (scales_hbm, scales),
            (points_hbm, points),
            (rank_hbm, rank),
            (tests.at[:split], front.at[line, odd, parity, spot, :split]),
            (tests.at[split:], back.at[line, spot, parity, odd]),
        ])
    ]
    for load in loads:
        load.start()
    for load in loads[:3]:
        load.wait()
    index = lax.broadcasted_iota(jnp.int32, points.shape, 0)
    scale = jnp.ones(points.shape, jnp.float32)
    for i in range(dims):
        scale = jnp.where(index == i, scales[i], scale)
    scaled = points[...] / scale
    side = jnp.where(rank[...] >= boundary[0], 1.0, 0.0)
    gap = jnp.zeros((-dims % 8, local), jnp.float32)
    high, mid, low = [jnp.concatenate([part, gap], axis=0) if dims % 8 else part for part in thirds(scaled)]
    norms = list(thirds(-0.5 * jnp.sum(scaled * scaled, axis=0, keepdims=True)))
    ones = [jnp.ones_like(side)] * 3
    info = jnp.concatenate([high, mid, low, side, 1.0 - side] + norms + ones, axis=0)
    wide = jnp.zeros((info.shape[0], tests.shape[1] - local), jnp.float32)
    front[line, odd, parity, spot, split:] = jnp.concatenate([info, wide], axis=1).astype(jnp.bfloat16)
    left[...] = jnp.concatenate(
        [high, high, mid, mid, low, jnp.zeros_like(low), high, -FAR * side, -FAR * (1.0 - side)] + ones + norms, axis=0
    ).T.astype(jnp.bfloat16)
    sample[...] = jnp.zeros_like(sample)
    for load in loads[3:]:
        load.wait()
    pl.semaphore_wait(barrier, half + 1 + above.astype(jnp.int32) + below.astype(jnp.int32))

    most = half - 1
    hops, jumps = lines + 1 + lines * most, lines * max(half, 2 * most)

    def send(kind, c, i):
        begin = 0 if kind < 2 else hops + (jumps if kind > 2 else 0)
        step = hops + jumps + lines * max(2, half)
        return s_all.at[c * step + begin + i + (lines + 1 if kind == 1 else 0)]

    def part(c, l):
        return back.at[l, spot, parity, odd] if c else front.at[l, odd, parity, spot]

    def along(c, l, down):
        return remote(part(c, l), part(c, l), send(0, c, jnp.where((l == line) & (down == 1), lines, l)), r_z.at[c, l], *there(line + 1 - 2 * down, odd, spot, parity))

    def to_mate(ref, send, recv):
        return remote(ref, ref, send, recv, *there(line, 1 - odd, spot, parity))

    def to_spot(ref, k, send, recv):
        return remote(ref, ref, send, recv, *there(line, odd, (spot + k) % half, parity))

    def hop(c, l):
        if c:
            return [to_mate(part(1, l), send(1, 1, l), r_a.at[1, l, 0])]
        return [to_spot(part(0, l), k, send(1, 0, l * most + k - 1), r_a.at[0, l, k - 1]) for k in range(1, half)]

    def leap(c, l, k):
        if c:
            return [
                to_spot(back.at[l, spot, parity, (odd + k) % 2], j, send(2, 1, l * 2 * most + k * most + j - 1), r_b.at[1, l, k * most + j - 1])
                for j in range(1, half)
            ]
        return [to_mate(front.at[l, odd, parity, (spot + half - k) % half], send(2, 0, l * half + k), r_b.at[0, l, k])]

    def leaps(c, l):
        return [copy for k in range(2 if c else half) for copy in leap(c, l, k)]

    def cross(c, l, j):
        ref = back.at[l, j, parity] if c else front.at[l, j, parity]
        return remote(ref, ref, send(3, c, l * (half if c else 2) + j), r_c.at[c, l, j], *there(line, odd, spot, 1 - parity))

    def go(copies):
        for copy in copies:
            copy.start()

    def come(copies):
        for copy in copies:
            copy.wait_recv()

    def leave(copies):
        for copy in copies:
            copy.wait_send()

    reach = jnp.minimum(line, lines - 1 - line)
    far = jnp.where(line < lines - 1 - line, 1, -1)

    def origin(n):
        return line + jnp.where(n <= 2 * reach, (2 * (n % 2) - 1) * ((n + 1) // 2), far * (n - reach))

    def upward(l):
        return (l <= line) & above

    def downward(l):
        return (l >= line) & below

    def arrive(n, own=False):
        l = origin(n)
        for c in range(2):
            if not own:
                along(c, l, 0).wait_recv()
            pl.when(upward(l))(along(c, l, 0).start)
            pl.when(downward(l))(along(c, l, 1).start)
            go(hop(c, l) + leap(c, l, 0))

    def meet(n):
        l = origin(n)
        for c in range(2):
            for k, copy in enumerate(hop(c, l), 1):
                copy.wait_recv()
                go(leap(c, l, k))
            cross(c, l, spot if c else odd).start()

    def add(l, p):
        terms = []
        for o in range(2):
            for s in range(half):
                pack = front[l, o, p, s]
                body, head, foot = pack[:split], pack[split : split + 16, :local], pack[split + 16 :, :local]
                right = jnp.concatenate([head, head, head, foot], axis=0)
                tile = jnp.exp(dot(left[...], right, ((1,), (0,)), None)).astype(jnp.bfloat16)
                test = jnp.concatenate([body, back[l, s, p, o]], axis=0)
                terms.append(dot(tile, test, ((1,), (0,)), None))
        while len(terms) > 1:
            terms = [a + b for a, b in zip(terms[::2], terms[1::2])] + terms[len(terms) // 2 * 2 :]
        sample[...] += terms[0]

    def close(n):
        l = origin(n)
        come(leaps(0, l))
        cross(0, l, 1 - odd).start()
        come(leaps(1, l))
        for k in range(1, half):
            cross(1, l, (spot + k) % half).start()

    def near(n):
        add(origin(n), parity)

    def last(n):
        l = origin(n)
        come([cross(0, l, j) for j in range(2)] + [cross(1, l, j) for j in range(half)])
        add(l, 1 - parity)

    def advance(n):
        arrive(n + 1)
        meet(n)

    arrive(0, True)
    each(0, lines - 1, advance)
    meet(lines - 1)
    close(0)

    def finish_line(n):
        close(n)
        near(n - 1)
        last(n - 1)

    each(1, lines, finish_line)
    near(lines - 1)
    last(lines - 1)
    def settle(l):
        for c in range(2):
            pl.when(upward(l))(along(c, l, 0).wait_send)
            pl.when(downward(l))(along(c, l, 1).wait_send)
            leave(hop(c, l) + leaps(c, l))
        leave([cross(0, l, j) for j in range(2)] + [cross(1, l, j) for j in range(half)])


    count = rows * half
    partner = col + 1 - 2 * parity
    total = sample[...]
    index = row * half + spot

    def place(i):
        return lax.div(i, half), 2 * lax.rem(i, half) + parity

    ranks = total.shape[1]

    def cut(ref, low):
        return ref.at[:, ranks // 2 :] if low else ref

    def cuts(ref, low):
        return ref.at[:, :, ranks // 2 :] if low else ref

    def mine_or(make, act):
        for low in range(2):
            pl.when(parity == low)(lambda low=low: act(make(low)))

    def other(make, act):
        for low in range(2):
            pl.when(parity == 1 - low)(lambda low=low: act(make(low)))

    def begin(copy):
        copy.start()

    def got(copy):
        copy.wait_recv()

    def sent(copy):
        copy.wait_send()

    def both(copy):
        copy.wait()

    square[...] = product(total, total, ((0,), (0,))).reshape(square.shape)

    def trade(low):
        return remote(cuts(square.at[low], low), cuts(mate, low), s_mate.at[0], r_mate.at[0], row, partner)

    other(trade, begin)
    each(0, lines, settle)
    mine_or(trade, got)
    mine[...] = square[parity] + mate[...]

    def scatter(k):
        there = lax.rem(index + k, count)
        r, c = place(there)
        return lambda low: remote(cut(mine.at[there], low), cut(piece.at[k], low), s_all.at[k], r_piece.at[k], r, c)

    each(1, count, lambda k: mine_or(scatter(k), begin))
    each(1, count, lambda k: mine_or(scatter(k), both))
    piece[0] = mine[index]
    done[...] = jnp.sum(piece[...], axis=0)
    gram[parity, index] = done[...]

    def collect(k):
        r, c = place(lax.rem(index + k, count))
        return lambda low: remote(cut(done, low), cut(gram.at[parity, index], low), s_all.at[k], r_done.at[k], r, c)

    def pass_on(k):
        there = lax.rem(index + count - k, count)

        def make(low):
            ref = cut(gram.at[low, there], low)
            return remote(ref, ref, s_all.at[count + k], r_over.at[k], row, partner)

        return make

    def relay(k):
        mine_or(collect(k), got)
        mine_or(pass_on(k), begin)

    def own(low):
        return remote(cut(done, low), cut(gram.at[low, index], low), s_all.at[count], r_over.at[0], row, partner)

    each(1, count, lambda k: mine_or(collect(k), begin))
    mine_or(own, begin)
    each(1, count, relay)
    mine_or(own, sent)
    other(own, got)

    def last_waits(k):
        mine_or(pass_on(k), sent)
        other(pass_on(k), got)
        mine_or(collect(k), sent)

    each(1, count, last_waits)
    other(trade, sent)


def far(x):
    return pltpu.with_memory_space_constraint(x, pltpu.HBM)


def sketch_gram(points, tests, rank, boundary, scales, rows, cols):
    local, ranks = tests.shape
    lines, half, count = rows // 2, cols // 2, rows * cols // 2
    lanes = 3 * (8 * ((points.shape[0] + 7) // 8)) + 8
    split = (local - lanes) // 32 * 16
    share = ranks // 2 // count
    f32 = jnp.float32
    dma = pltpu.SemaphoreType.DMA
    wide, most = max(2, half), half - 1
    sample, gram = pl.pallas_call(
        functools.partial(sample_kernel, rows, cols),
        out_shape=(
            jax.ShapeDtypeStruct((local, ranks), f32),
            jax.ShapeDtypeStruct((2, count, share, ranks), f32),
        ),
        in_specs=[HBM, HBM, HBM, SMEM, HBM],
        out_specs=(VMEM, VMEM),
        scratch_shapes=[
            pltpu.VMEM((lines, 2, 2, half, split + lanes, ranks), tests.dtype),
            pltpu.VMEM((lines, half, 2, 2, local - split, ranks), tests.dtype),
            pltpu.VMEM((local, 2 * lanes), tests.dtype),
            pltpu.VMEM(points.shape, f32), pltpu.VMEM((1, local), rank.dtype), pltpu.SMEM(scales.shape, f32), dma((5,)),
            pltpu.VMEM((2, count, share, ranks), f32),
            pltpu.VMEM((count, share, ranks), f32),
            pltpu.VMEM((count, share, ranks), f32),
            pltpu.VMEM((count, share, ranks), f32),
            pltpu.VMEM((share, ranks), f32),
            dma((max(2 * (lines + 1 + lines * most + lines * max(half, 2 * most) + lines * wide), 2 * count),)),
            dma((2, lines)), dma((2, lines, most)), dma((2, lines, max(half, 2 * most))), dma((2, lines, wide)),
            dma((1,)), dma((1,)), dma((count,)), dma((count,)), dma((count,)),
        ],
        compiler_params=pltpu.CompilerParams(
            collective_id=0,
            has_side_effects=True,
            vmem_limit_bytes=2 * rows * cols * (local + lanes) * ranks + 8 * 2**20,
        ),
        name="sketch_gram",
    )(far(points), far(tests), far(rank[None]), boundary, far(scales))
    return sample, gram.reshape(ranks, ranks)


def tree(parts):
    while len(parts) > 1:
        parts = [p + q for p, q in zip(parts[::2], parts[1::2])] + parts[len(parts) // 2 * 2 :]
    return parts[0]


def sixfold(a, b):
    ah, am, al = thirds(a)
    bh, bm, bl = thirds(b)
    return jnp.concatenate([ah, ah, am, ah, al, am], axis=0), jnp.concatenate([bh, bm, bh, bl, bh, bm], axis=0)


def factor_block(a, zero):
    size, wide, width = a.shape[0], 8, 32
    shape = (wide, size)
    lane = lax.broadcasted_iota(jnp.int32, shape, 1)
    line = lax.broadcasted_iota(jnp.int32, shape, 0)

    def spread(x):
        return jnp.broadcast_to(x, shape)

    def column(x, at):
        return jnp.take_along_axis(x, zero + at, axis=1, mode="promise_in_bounds")

    rest = a
    upper, inverse = [], []
    for begin in range(0, size, width):
        end = begin + width
        blocks = [rest[i : i + wide] for i in range(0, width, wide)]
        us, ms = [], []
        marks = [column(blocks[0], begin + u) for u in range(wide)]
        for at in range(begin, end, wide):
            inside = (lane >= at) & (lane < at + wide)
            x = blocks.pop(0)
            z = jnp.where(inside, jnp.where(lane - at == line, 1.0, 0.0), x)
            y = z
            old = [[column(block, at + t) for t in range(wide)] for block in blocks]
            ahead = [column(x, at + wide + u) for u in range(wide)] if blocks else []
            fresh = [column(blocks[0], at + wide + u) for u in range(wide)] if blocks else []
            over, root = jnp.zeros(shape, jnp.float32), jnp.zeros(shape, jnp.float32)
            for s in range(wide):
                pivot = spread(marks[s][s : s + 1])
                inv = 1.0 / pivot
                over = jnp.where(line == s, inv, over)
                root = jnp.where(line == s, pivot, root)
                ratio = marks[s] * inv
                low = jnp.where(line > s, ratio, 0.0)
                both = jnp.where(line == s, 0.0, ratio)
                for u in range(s + 1, wide):
                    marks[u] = marks[u] - both * spread(marks[u][s : s + 1])
                ahead = [c - both * spread(c[s : s + 1]) for c in ahead]
                if s + 1 < wide:
                    x = x - low * spread(x[s : s + 1])
                    y = y - low * spread(y[s : s + 1])
                z = z - both * spread(z[s : s + 1])
            ahead = [c * over for c in ahead]
            marks = [
                f - tree([old[0][t] * spread(c[t : t + 1]) for t in range(wide)]) for f, c in zip(fresh, ahead)
            ]
            z = z * over
            rows = [spread(z[t : t + 1]) for t in range(wide)]
            blocks = [
                jnp.where(inside, 0.0, block) - tree([c * r for c, r in zip(columns, rows)])
                for block, columns in zip(blocks, old)
            ]
            root = lax.rsqrt(root)
            us.append(jnp.where(lane >= at + line, x * root, 0.0))
            ms.append(jnp.where(lane <= at + line, y * root, 0.0))
        u, m = jnp.concatenate(us, axis=0), jnp.concatenate(ms, axis=0)
        upper.append(u)
        inverse.append(m)
        if end < size:
            left, right = sixfold(u, jnp.where(lax.broadcasted_iota(jnp.int32, u.shape, 1) >= end, u, m))
            change = dot(left.T[end:].astype(jnp.bfloat16), right.astype(jnp.bfloat16), ((1,), (0,)), None)
            spot = lax.broadcasted_iota(jnp.int32, change.shape, 1)
            rest = jnp.where((spot >= begin) & (spot < end), 0.0, rest[width:]) - change
    return jnp.concatenate(upper, axis=0), jnp.concatenate(inverse, axis=0)


def product(a, b, dims):
    (i,), (j,) = dims
    ah, am, al = [part.astype(jnp.bfloat16) for part in thirds(a)]
    bh, bm, bl = [part.astype(jnp.bfloat16) for part in thirds(b)]
    return dot(jnp.concatenate([ah, ah, am, ah, al, am], axis=i), jnp.concatenate([bh, bm, bh, bl, bh, bm], axis=j), dims, None)


def finish_kernel(scale, gram, sample, basis, factor):
    half = gram.shape[0] // 2
    head, cross, foot = [part * scale for part in (gram[:half, :half], gram[:half, half:], gram[half:, half:])]
    same = lax.broadcasted_iota(jnp.int32, (half, half), 0) == lax.broadcasted_iota(jnp.int32, (half, half), 1)
    trace = jnp.sum(jnp.sum(jnp.where(same, head + foot, 0.0), axis=0, keepdims=True), axis=1, keepdims=True)
    shift = jnp.where(same, (0.05 / half) * trace, 0.0)
    zero = (head[:8] * 0.0).astype(jnp.int32)
    up, low = factor_block(head + shift, zero)
    lift = product(low, cross, ((1,), (0,)))
    up2, low2 = factor_block(foot + shift - product(lift.T, lift, ((1,), (0,))), zero)
    first = product(sample[:, :half], low, ((1,), (1,)))
    rest = sample[:, half:] - product(first, lift, ((1,), (0,)))
    basis[:, :half] = first
    basis[:, half:] = product(rest, low2, ((1,), (1,)))
    factor[:half, :half] = up.T
    factor[:half, half:] = jnp.zeros((half, half), jnp.float32)
    factor[half:, :half] = lift.T
    factor[half:, half:] = up2.T


def finish(gram, sample, everyone):
    return pl.pallas_call(
        functools.partial(finish_kernel, 1.0 / everyone),
        out_shape=(
            jax.ShapeDtypeStruct(sample.shape, jnp.float32),
            jax.ShapeDtypeStruct(gram.shape, jnp.float32),
        ),
        in_specs=[VMEM, VMEM],
        out_specs=(VMEM, VMEM),
        compiler_params=pltpu.CompilerParams(vmem_limit_bytes=8 * 2**20),
        name="finish",
    )(gram, sample)


def body(rows, cols, points, sketch, rank, boundary, scales):
    sample, gram = sketch_gram(points, sketch, rank, boundary, scales, rows, cols)
    return finish(gram, sample, rows * cols * points.shape[1])


def solution(mesh):
    placed = (P(None, ("row", "col")), P(("row", "col"), None), P(("row", "col")), P(), P())
    return jax.shard_map(
        functools.partial(body, mesh.shape["row"], mesh.shape["col"]),
        mesh=mesh,
        in_specs=placed,
        out_specs=(P(("row", "col"), None), P()),
        check_vma=False,
    )
```

```python
import functools

import jax
import jax.numpy as jnp
from jax import lax
from jax.experimental import pallas as pl
from jax.experimental.pallas import tpu as pltpu
from jax.sharding import PartitionSpec as P

HIGHEST = lax.Precision.HIGHEST
FAR = 4992.0
VMEM = pl.BlockSpec(memory_space=pltpu.VMEM)
SMEM = pl.BlockSpec(memory_space=pltpu.SMEM)
HBM = pl.BlockSpec(memory_space=pltpu.HBM)


def dot(a, b, dims, precision=HIGHEST):
    return lax.dot_general(
        a, b, (dims, ((), ())), precision=precision, preferred_element_type=jnp.float32
    )


def remote(src, dst, send, recv, row, col):
    return pltpu.make_async_remote_copy(
        src_ref=src,
        dst_ref=dst,
        send_sem=send,
        recv_sem=recv,
        device_id=(row, col),
        device_id_type=pl.DeviceIdType.MESH,
    )


def each(start, stop, step):
    def run(index, carry):
        step(index)
        return carry

    lax.fori_loop(start, stop, run, 0)


def thirds(x):
    high = x.astype(jnp.bfloat16).astype(jnp.float32)
    mid = (x - high).astype(jnp.bfloat16).astype(jnp.float32)
    return high, mid, (x - high - mid).astype(jnp.bfloat16).astype(jnp.float32)


def sample_kernel(
    rows, cols, points_hbm, tests, rank_hbm, boundary, scales_hbm, sample, gram, front, back, left,
    points, rank, scales, s_in, square, mate, mine, piece, done,
    s_all, r_z, r_a, r_b, r_c, s_mate, r_mate, r_piece, r_done, r_over,
):
    row, col = lax.axis_index("row"), lax.axis_index("col")
    lines, half = rows // 2, cols // 2
    line, odd = row // 2, row % 2
    spot, parity = col // 2, col % 2
    local = tests.shape[0]
    split = local - back.shape[-2]
    dims = points.shape[0]
    mesh = pl.DeviceIdType.MESH
    above, below = line < lines - 1, line > 0

    def there(l, o, s, p):
        return 2 * l + o, 2 * s + p

    barrier = pltpu.get_barrier_semaphore()

    def greet(l, o, s, p):
        pl.semaphore_signal(barrier, 1, device_id=there(l, o, s, p), device_id_type=mesh)

    @pl.when(above)
    def _():
        greet(line + 1, odd, spot, parity)

    @pl.when(below)
    def _():
        greet(line - 1, odd, spot, parity)

    for k in range(1, half):
        greet(line, odd, (spot + k) % half, parity)
    greet(line, 1 - odd, spot, parity)
    greet(line, odd, spot, 1 - parity)

    loads = [
        pltpu.make_async_copy(src, dst, s_in.at[i])
        for i, (src, dst) in enumerate([
            (scales_hbm, scales),
            (points_hbm, points),
            (rank_hbm, rank),
            (tests.at[:split], front.at[line, odd, parity, spot, :split]),
            (tests.at[split:], back.at[line, spot, parity, odd]),
        ])
    ]
    for load in loads:
        load.start()
    for load in loads[:3]:
        load.wait()
    index = lax.broadcasted_iota(jnp.int32, points.shape, 0)
    scale = jnp.ones(points.shape, jnp.float32)
    for i in range(dims):
        scale = jnp.where(index == i, scales[i], scale)
    scaled = points[...] / scale
    side = jnp.where(rank[...] >= boundary[0], 1.0, 0.0)
    gap = jnp.zeros((-dims % 8, local), jnp.float32)
    high, mid, low = [jnp.concatenate([part, gap], axis=0) if dims % 8 else part for part in thirds(scaled)]
    norms = list(thirds(-0.5 * jnp.sum(scaled * scaled, axis=0, keepdims=True)))
    ones = [jnp.ones_like(side)] * 3
    info = jnp.concatenate([high, mid, low, side, 1.0 - side] + norms + ones, axis=0)
    wide = jnp.zeros((info.shape[0], tests.shape[1] - local), jnp.float32)
    front[line, odd, parity, spot, split:] = jnp.concatenate([info, wide], axis=1).astype(jnp.bfloat16)
    left[...] = jnp.concatenate(
        [high, high, mid, mid, low, jnp.zeros_like(low), high, -FAR * side, -FAR * (1.0 - side)] + ones + norms, axis=0
    ).T.astype(jnp.bfloat16)
    sample[...] = jnp.zeros_like(sample)
    for load in loads[3:]:
        load.wait()
    pl.semaphore_wait(barrier, half + 1 + above.astype(jnp.int32) + below.astype(jnp.int32))

    most = half - 1
    hops, jumps = lines + 1 + lines * most, lines * max(half, 2 * most)

    def send(kind, c, i):
        begin = 0 if kind < 2 else hops + (jumps if kind > 2 else 0)
        step = hops + jumps + lines * max(2, half)
        return s_all.at[c * step + begin + i + (lines + 1 if kind == 1 else 0)]

    def part(c, l):
        return back.at[l, spot, parity, odd] if c else front.at[l, odd, parity, spot]

    def along(c, l, down):
        return remote(part(c, l), part(c, l), send(0, c, jnp.where((l == line) & (down == 1), lines, l)), r_z.at[c, l], *there(line + 1 - 2 * down, odd, spot, parity))

    def to_mate(ref, send, recv):
        return remote(ref, ref, send, recv, *there(line, 1 - odd, spot, parity))

    def to_spot(ref, k, send, recv):
        return remote(ref, ref, send, recv, *there(line, odd, (spot + k) % half, parity))

    def hop(c, l):
        if c:
            return [to_mate(part(1, l), send(1, 1, l), r_a.at[1, l, 0])]
        return [to_spot(part(0, l), k, send(1, 0, l * most + k - 1), r_a.at[0, l, k - 1]) for k in range(1, half)]

    def leap(c, l, k):
        if c:
            return [
                to_spot(back.at[l, spot, parity, (odd + k) % 2], j, send(2, 1, l * 2 * most + k * most + j - 1), r_b.at[1, l])
                for j in range(1, half)
            ]
        return [to_mate(front.at[l, odd, parity, (spot + half - k) % half], send(2, 0, l * half + k), r_b.at[0, l])]

    def leaps(c, l):
        return [copy for k in range(2 if c else half) for copy in leap(c, l, k)]

    def cross(c, l, j):
        ref = back.at[l, j, parity] if c else front.at[l, j, parity]
        return remote(ref, ref, send(3, c, l * (half if c else 2) + j), r_c.at[c, l], *there(line, odd, spot, 1 - parity))

    def go(copies):
        for copy in copies:
            copy.start()

    def come(copies):
        for copy in copies:
            copy.wait_recv()

    def leave(copies):
        for copy in copies:
            copy.wait_send()

    reach = jnp.minimum(line, lines - 1 - line)
    far = jnp.where(line < lines - 1 - line, 1, -1)

    def origin(n):
        return line + jnp.where(n <= 2 * reach, (2 * (n % 2) - 1) * ((n + 1) // 2), far * (n - reach))

    def upward(l):
        return (l <= line) & above

    def downward(l):
        return (l >= line) & below

    def arrive(n, own=False):
        l = origin(n)
        for c in range(2):
            if not own:
                along(c, l, 0).wait_recv()
            pl.when(upward(l))(along(c, l, 0).start)
            pl.when(downward(l))(along(c, l, 1).start)
            go(hop(c, l) + leap(c, l, 0))

    def meet(n):
        l = origin(n)
        for c in range(2):
            for k, copy in enumerate(hop(c, l), 1):
                copy.wait_recv()
                go(leap(c, l, k))
            cross(c, l, spot if c else odd).start()

    def add(l, p):
        terms = []
        for o in range(2):
            for s in range(half):
                pack = front[l, o, p, s]
                body, head, foot = pack[:split], pack[split : split + 16, :local], pack[split + 16 :, :local]
                right = jnp.concatenate([head, head, head, foot], axis=0)
                tile = jnp.exp(dot(left[...], right, ((1,), (0,)), None)).astype(jnp.bfloat16)
                test = jnp.concatenate([body, back[l, s, p, o]], axis=0)
                terms.append(dot(tile, test, ((1,), (0,)), None))
        while len(terms) > 1:
            terms = [a + b for a, b in zip(terms[::2], terms[1::2])] + terms[len(terms) // 2 * 2 :]
        sample[...] += terms[0]

    def landed(ref, recv):
        remote(ref, ref, s_all.at[0], recv, row, col + 1 - 2 * parity).wait_recv()

    def close(n):
        l = origin(n)
        landed(front.at[l, 1 - odd, parity], r_b.at[0, l])
        cross(0, l, 1 - odd).start()
        landed(back.at[l, :most, parity], r_b.at[1, l])
        for k in range(1, half):
            cross(1, l, (spot + k) % half).start()

    def near(n):
        add(origin(n), parity)

    def last(n):
        l = origin(n)
        landed(front.at[l, :, 1 - parity], r_c.at[0, l])
        landed(back.at[l, :, 1 - parity], r_c.at[1, l])
        add(l, 1 - parity)

    def advance(n):
        arrive(n + 1)
        meet(n)

    arrive(0, True)
    each(0, lines - 1, advance)
    meet(lines - 1)
    close(0)

    def finish_line(n):
        close(n)
        near(n - 1)
        last(n - 1)

    each(1, lines, finish_line)
    near(lines - 1)
    last(lines - 1)
    def settle(l):
        for c in range(2):
            pl.when(upward(l))(along(c, l, 0).wait_send)
            pl.when(downward(l))(along(c, l, 1).wait_send)
            leave(hop(c, l) + leaps(c, l))
        leave([cross(0, l, j) for j in range(2)] + [cross(1, l, j) for j in range(half)])


    count = rows * half
    partner = col + 1 - 2 * parity
    total = sample[...]
    index = row * half + spot

    def place(i):
        return lax.div(i, half), 2 * lax.rem(i, half) + parity

    ranks = total.shape[1]

    def cut(ref, low):
        return ref.at[:, ranks // 2 :] if low else ref

    def cuts(ref, low):
        return ref.at[:, :, ranks // 2 :] if low else ref

    def mine_or(make, act):
        for low in range(2):
            pl.when(parity == low)(lambda low=low: act(make(low)))

    def other(make, act):
        for low in range(2):
            pl.when(parity == 1 - low)(lambda low=low: act(make(low)))

    def begin(copy):
        copy.start()

    def got(copy):
        copy.wait_recv()

    def sent(copy):
        copy.wait_send()

    def both(copy):
        copy.wait()

    square[...] = product(total, total, ((0,), (0,))).reshape(square.shape)

    def trade(low):
        return remote(cuts(square.at[low], low), cuts(mate, low), s_mate.at[0], r_mate.at[0], row, partner)

    other(trade, begin)
    each(0, lines, settle)
    mine_or(trade, got)
    mine[...] = square[parity] + mate[...]

    def scatter(k):
        there = lax.rem(index + k, count)
        r, c = place(there)
        return lambda low: remote(cut(mine.at[there], low), cut(piece.at[k], low), s_all.at[k], r_piece.at[0], r, c)

    each(1, count, lambda k: mine_or(scatter(k), begin))
    def pieces(low):
        ref = cuts(piece.at[1:], low)
        return remote(ref, ref, s_all.at[0], r_piece.at[0], row, partner)

    mine_or(pieces, got)
    piece[0] = mine[index]
    done[...] = jnp.sum(piece[...], axis=0)
    gram[parity, index] = done[...]

    def collect(k):
        r, c = place(lax.rem(index + k, count))
        return lambda low: remote(cut(done, low), cut(gram.at[parity, index], low), s_all.at[count + k], r_done.at[0], r, c)

    def rest(low):
        ref = cuts(gram.at[low, 1:], low)
        return remote(ref, ref, s_all.at[0], r_done.at[0], row, partner)

    def pass_on(low):
        ref = cuts(gram.at[low], low)
        return remote(ref, ref, s_all.at[0], r_over.at[0], row, partner)

    each(1, count, lambda k: mine_or(collect(k), begin))
    each(1, count, lambda k: mine_or(scatter(k), sent))
    mine_or(rest, got)
    mine_or(pass_on, begin)
    each(1, count, lambda k: mine_or(collect(k), sent))
    mine_or(pass_on, sent)
    other(pass_on, got)
    other(trade, sent)


def far(x):
    return pltpu.with_memory_space_constraint(x, pltpu.HBM)


def sketch_gram(points, tests, rank, boundary, scales, rows, cols):
    local, ranks = tests.shape
    lines, half, count = rows // 2, cols // 2, rows * cols // 2
    lanes = 3 * (8 * ((points.shape[0] + 7) // 8)) + 8
    split = (local - lanes) // 32 * 16
    share = ranks // 2 // count
    f32 = jnp.float32
    dma = pltpu.SemaphoreType.DMA
    wide, most = max(2, half), half - 1
    sample, gram = pl.pallas_call(
        functools.partial(sample_kernel, rows, cols),
        out_shape=(
            jax.ShapeDtypeStruct((local, ranks), f32),
            jax.ShapeDtypeStruct((2, count, share, ranks), f32),
        ),
        in_specs=[HBM, HBM, HBM, SMEM, HBM],
        out_specs=(VMEM, VMEM),
        scratch_shapes=[
            pltpu.VMEM((lines, 2, 2, half, split + lanes, ranks), tests.dtype),
            pltpu.VMEM((lines, half, 2, 2, local - split, ranks), tests.dtype),
            pltpu.VMEM((local, 2 * lanes), tests.dtype),
            pltpu.VMEM(points.shape, f32), pltpu.VMEM((1, local), rank.dtype), pltpu.SMEM(scales.shape, f32), dma((5,)),
            pltpu.VMEM((2, count, share, ranks), f32),
            pltpu.VMEM((count, share, ranks), f32),
            pltpu.VMEM((count, share, ranks), f32),
            pltpu.VMEM((count, share, ranks), f32),
            pltpu.VMEM((share, ranks), f32),
            dma((max(2 * (lines + 1 + lines * most + lines * max(half, 2 * most) + lines * wide), 2 * count),)),
            dma((2, lines)), dma((2, lines, most)), dma((2, lines)), dma((2, lines)),
            dma((1,)), dma((1,)), dma((1,)), dma((1,)), dma((1,)),
        ],
        compiler_params=pltpu.CompilerParams(
            collective_id=0,
            has_side_effects=True,
            vmem_limit_bytes=2 * rows * cols * (local + lanes) * ranks + 8 * 2**20,
        ),
        name="sketch_gram",
    )(far(points), far(tests), far(rank[None]), boundary, far(scales))
    return sample, gram.reshape(ranks, ranks)


def tree(parts):
    while len(parts) > 1:
        parts = [p + q for p, q in zip(parts[::2], parts[1::2])] + parts[len(parts) // 2 * 2 :]
    return parts[0]


def sixfold(a, b):
    ah, am, al = thirds(a)
    bh, bm, bl = thirds(b)
    return jnp.concatenate([ah, ah, am, ah, al, am], axis=0), jnp.concatenate([bh, bm, bh, bl, bh, bm], axis=0)


def factor_block(a, zero):
    size, wide, width = a.shape[0], 8, 32
    shape = (wide, size)
    lane = lax.broadcasted_iota(jnp.int32, shape, 1)
    line = lax.broadcasted_iota(jnp.int32, shape, 0)

    def spread(x):
        return jnp.broadcast_to(x, shape)

    def column(x, at):
        return jnp.take_along_axis(x, zero + at, axis=1, mode="promise_in_bounds")

    rest = a
    upper, inverse = [], []
    for begin in range(0, size, width):
        end = begin + width
        blocks = [rest[i : i + wide] for i in range(0, width, wide)]
        us, ms = [], []
        marks = [column(blocks[0], begin + u) for u in range(wide)]
        for at in range(begin, end, wide):
            inside = (lane >= at) & (lane < at + wide)
            x = blocks.pop(0)
            z = jnp.where(inside, jnp.where(lane - at == line, 1.0, 0.0), x)
            y = z
            old = [[column(block, at + t) for t in range(wide)] for block in blocks]
            ahead = [column(x, at + wide + u) for u in range(wide)] if blocks else []
            fresh = [column(blocks[0], at + wide + u) for u in range(wide)] if blocks else []
            over, root = jnp.zeros(shape, jnp.float32), jnp.zeros(shape, jnp.float32)
            for s in range(wide):
                pivot = spread(marks[s][s : s + 1])
                inv = 1.0 / pivot
                over = jnp.where(line == s, inv, over)
                root = jnp.where(line == s, pivot, root)
                ratio = marks[s] * inv
                low = jnp.where(line > s, ratio, 0.0)
                both = jnp.where(line == s, 0.0, ratio)
                for u in range(s + 1, wide):
                    marks[u] = marks[u] - both * spread(marks[u][s : s + 1])
                ahead = [c - both * spread(c[s : s + 1]) for c in ahead]
                if s + 1 < wide:
                    x = x - low * spread(x[s : s + 1])
                    y = y - low * spread(y[s : s + 1])
                z = z - both * spread(z[s : s + 1])
            ahead = [c * over for c in ahead]
            marks = [
                f - tree([old[0][t] * spread(c[t : t + 1]) for t in range(wide)]) for f, c in zip(fresh, ahead)
            ]
            z = z * over
            rows = [spread(z[t : t + 1]) for t in range(wide)]
            blocks = [
                jnp.where(inside, 0.0, block) - tree([c * r for c, r in zip(columns, rows)])
                for block, columns in zip(blocks, old)
            ]
            root = lax.rsqrt(root)
            us.append(jnp.where(lane >= at + line, x * root, 0.0))
            ms.append(jnp.where(lane <= at + line, y * root, 0.0))
        u, m = jnp.concatenate(us, axis=0), jnp.concatenate(ms, axis=0)
        upper.append(u)
        inverse.append(m)
        if end < size:
            left, right = sixfold(u, jnp.where(lax.broadcasted_iota(jnp.int32, u.shape, 1) >= end, u, m))
            change = dot(left.T[end:].astype(jnp.bfloat16), right.astype(jnp.bfloat16), ((1,), (0,)), None)
            spot = lax.broadcasted_iota(jnp.int32, change.shape, 1)
            rest = jnp.where((spot >= begin) & (spot < end), 0.0, rest[width:]) - change
    return jnp.concatenate(upper, axis=0), jnp.concatenate(inverse, axis=0)


def product(a, b, dims):
    (i,), (j,) = dims
    ah, am, al = [part.astype(jnp.bfloat16) for part in thirds(a)]
    bh, bm, bl = [part.astype(jnp.bfloat16) for part in thirds(b)]
    return dot(jnp.concatenate([ah, ah, am, ah, al, am], axis=i), jnp.concatenate([bh, bm, bh, bl, bh, bm], axis=j), dims, None)


def finish_kernel(scale, gram, sample, basis, factor):
    half = gram.shape[0] // 2
    head, cross, foot = [part * scale for part in (gram[:half, :half], gram[:half, half:], gram[half:, half:])]
    same = lax.broadcasted_iota(jnp.int32, (half, half), 0) == lax.broadcasted_iota(jnp.int32, (half, half), 1)
    trace = jnp.sum(jnp.sum(jnp.where(same, head + foot, 0.0), axis=0, keepdims=True), axis=1, keepdims=True)
    shift = jnp.where(same, (0.05 / half) * trace, 0.0)
    zero = (head[:8] * 0.0).astype(jnp.int32)
    up, low = factor_block(head + shift, zero)
    lift = product(low, cross, ((1,), (0,)))
    up2, low2 = factor_block(foot + shift - product(lift.T, lift, ((1,), (0,))), zero)
    first = product(sample[:, :half], low, ((1,), (1,)))
    rest = sample[:, half:] - product(first, lift, ((1,), (0,)))
    basis[:, :half] = first
    basis[:, half:] = product(rest, low2, ((1,), (1,)))
    factor[:half, :half] = up.T
    factor[:half, half:] = jnp.zeros((half, half), jnp.float32)
    factor[half:, :half] = lift.T
    factor[half:, half:] = up2.T


def finish(gram, sample, everyone):
    return pl.pallas_call(
        functools.partial(finish_kernel, 1.0 / everyone),
        out_shape=(
            jax.ShapeDtypeStruct(sample.shape, jnp.float32),
            jax.ShapeDtypeStruct(gram.shape, jnp.float32),
        ),
        in_specs=[VMEM, VMEM],
        out_specs=(VMEM, VMEM),
        compiler_params=pltpu.CompilerParams(vmem_limit_bytes=8 * 2**20),
        name="finish",
    )(gram, sample)


def body(rows, cols, points, sketch, rank, boundary, scales):
    sample, gram = sketch_gram(points, sketch, rank, boundary, scales, rows, cols)
    return finish(gram, sample, rows * cols * points.shape[1])


def solution(mesh):
    placed = (P(None, ("row", "col")), P(("row", "col"), None), P(("row", "col")), P(), P())
    return jax.shard_map(
        functools.partial(body, mesh.shape["row"], mesh.shape["col"]),
        mesh=mesh,
        in_specs=placed,
        out_specs=(P(("row", "col"), None), P()),
        check_vma=False,
    )
```

```python
import functools

import jax
import jax.numpy as jnp
from jax import lax
from jax.experimental import pallas as pl
from jax.experimental.pallas import tpu as pltpu
from jax.sharding import PartitionSpec as P

HIGHEST = lax.Precision.HIGHEST
FAR = 4992.0
VMEM = pl.BlockSpec(memory_space=pltpu.VMEM)
SMEM = pl.BlockSpec(memory_space=pltpu.SMEM)
HBM = pl.BlockSpec(memory_space=pltpu.HBM)


def dot(a, b, dims, precision=HIGHEST):
    return lax.dot_general(
        a, b, (dims, ((), ())), precision=precision, preferred_element_type=jnp.float32
    )


def remote(src, dst, send, recv, row, col):
    return pltpu.make_async_remote_copy(
        src_ref=src,
        dst_ref=dst,
        send_sem=send,
        recv_sem=recv,
        device_id=(row, col),
        device_id_type=pl.DeviceIdType.MESH,
    )


def each(start, stop, step):
    def run(index, carry):
        step(index)
        return carry

    lax.fori_loop(start, stop, run, 0)


def thirds(x):
    high = x.astype(jnp.bfloat16).astype(jnp.float32)
    mid = (x - high).astype(jnp.bfloat16).astype(jnp.float32)
    return high, mid, (x - high - mid).astype(jnp.bfloat16).astype(jnp.float32)


def sample_kernel(
    rows, cols, points_hbm, tests, rank_hbm, boundary, scales_hbm, sample, gram, front, back, left,
    points, rank, scales, s_in, square, mate, mine, piece, done,
    s_all, r_z, r_a, r_b, r_c, s_mate, r_mate, r_piece, r_done, r_over,
):
    row, col = lax.axis_index("row"), lax.axis_index("col")
    lines, half = rows // 2, cols // 2
    line, odd = row // 2, row % 2
    spot, parity = col // 2, col % 2
    local = tests.shape[0]
    split = local - back.shape[-2]
    dims = points.shape[0]
    mesh = pl.DeviceIdType.MESH
    above, below = line < lines - 1, line > 0

    def there(l, o, s, p):
        return 2 * l + o, 2 * s + p

    barrier = pltpu.get_barrier_semaphore()

    def greet(l, o, s, p):
        pl.semaphore_signal(barrier, 1, device_id=there(l, o, s, p), device_id_type=mesh)

    @pl.when(above)
    def _():
        greet(line + 1, odd, spot, parity)

    @pl.when(below)
    def _():
        greet(line - 1, odd, spot, parity)

    for k in range(1, half):
        greet(line, odd, (spot + k) % half, parity)
    greet(line, 1 - odd, spot, parity)
    greet(line, odd, spot, 1 - parity)

    loads = [
        pltpu.make_async_copy(src, dst, s_in.at[i])
        for i, (src, dst) in enumerate([
            (scales_hbm, scales),
            (points_hbm, points),
            (rank_hbm, rank),
            (tests.at[:split], front.at[line, odd, parity, spot, :split]),
            (tests.at[split:], back.at[line, spot, parity, odd]),
        ])
    ]
    for load in loads:
        load.start()
    for load in loads[:3]:
        load.wait()
    index = lax.broadcasted_iota(jnp.int32, points.shape, 0)
    scale = jnp.ones(points.shape, jnp.float32)
    for i in range(dims):
        scale = jnp.where(index == i, scales[i], scale)
    scaled = points[...] / scale
    side = jnp.where(rank[...] >= boundary[0], 1.0, 0.0)
    gap = jnp.zeros((-dims % 8, local), jnp.float32)
    high, mid, low = [jnp.concatenate([part, gap], axis=0) if dims % 8 else part for part in thirds(scaled)]
    norms = list(thirds(-0.5 * jnp.sum(scaled * scaled, axis=0, keepdims=True)))
    ones = [jnp.ones_like(side)] * 3
    info = jnp.concatenate([high, mid, low, side, 1.0 - side] + norms + ones, axis=0)
    wide = jnp.zeros((info.shape[0], tests.shape[1] - local), jnp.float32)
    front[line, odd, parity, spot, split:] = jnp.concatenate([info, wide], axis=1).astype(jnp.bfloat16)
    left[...] = jnp.concatenate(
        [high, high, mid, mid, low, jnp.zeros_like(low), high, -FAR * side, -FAR * (1.0 - side)] + ones + norms, axis=0
    ).T.astype(jnp.bfloat16)
    sample[...] = jnp.zeros_like(sample)
    for load in loads[3:]:
        load.wait()
    pl.semaphore_wait(barrier, half + 1 + above.astype(jnp.int32) + below.astype(jnp.int32))

    most = half - 1
    hops, jumps = lines + 1 + lines * most, lines * max(half, 2 * most)

    def send(kind, c, i):
        begin = 0 if kind < 2 else hops + (jumps if kind > 2 else 0)
        step = hops + jumps + lines * max(2, half)
        return s_all.at[c * step + begin + i + (lines + 1 if kind == 1 else 0)]

    def part(c, l):
        return back.at[l, spot, parity, odd] if c else front.at[l, odd, parity, spot]

    def along(c, l, down):
        return remote(part(c, l), part(c, l), send(0, c, jnp.where((l == line) & (down == 1), lines, l)), r_z.at[c, l], *there(line + 1 - 2 * down, odd, spot, parity))

    def to_mate(ref, send, recv):
        return remote(ref, ref, send, recv, *there(line, 1 - odd, spot, parity))

    def to_spot(ref, k, send, recv):
        return remote(ref, ref, send, recv, *there(line, odd, (spot + k) % half, parity))

    def hop(c, l):
        if c:
            return [to_mate(part(1, l), send(1, 1, l), r_a.at[1, l, 0])]
        return [to_spot(part(0, l), k, send(1, 0, l * most + k - 1), r_a.at[0, l, k - 1]) for k in range(1, half)]

    def leap(c, l, k):
        if c:
            return [
                to_spot(back.at[l, spot, parity, (odd + k) % 2], j, send(2, 1, l * 2 * most + k * most + j - 1), r_b.at[1, l])
                for j in range(1, half)
            ]
        return [to_mate(front.at[l, odd, parity, (spot + half - k) % half], send(2, 0, l * half + k), r_b.at[0, l])]

    def leaps(c, l):
        return [copy for k in range(2 if c else half) for copy in leap(c, l, k)]

    def cross(c, l, j):
        ref = back.at[l, j, parity] if c else front.at[l, j, parity]
        return remote(ref, ref, send(3, c, l * (half if c else 2) + j), r_c.at[c, l], *there(line, odd, spot, 1 - parity))

    def go(copies):
        for copy in copies:
            copy.start()

    def come(copies):
        for copy in copies:
            copy.wait_recv()

    def leave(copies):
        for copy in copies:
            copy.wait_send()

    reach = jnp.minimum(line, lines - 1 - line)
    far = jnp.where(line < lines - 1 - line, 1, -1)

    def origin(n):
        return line + jnp.where(n <= 2 * reach, (2 * (n % 2) - 1) * ((n + 1) // 2), far * (n - reach))

    def upward(l):
        return (l <= line) & above

    def downward(l):
        return (l >= line) & below

    def arrive(n, own=False):
        l = origin(n)
        for c in range(2):
            if not own:
                along(c, l, 0).wait_recv()
            pl.when(upward(l))(along(c, l, 0).start)
            pl.when(downward(l))(along(c, l, 1).start)
            go(hop(c, l) + leap(c, l, 0))

    def meet(n):
        l = origin(n)
        for c in range(2):
            for k, copy in enumerate(hop(c, l), 1):
                copy.wait_recv()
                go(leap(c, l, k))
            cross(c, l, spot if c else odd).start()

    def add(l, p, gate=None):
        places = [(o, s) for o in range(2) for s in range(half)]
        tiles = []
        for o, s in places:
            head, foot = front[l, o, p, s, split : split + 16, :local], front[l, o, p, s, split + 16 :, :local]
            right = jnp.concatenate([head, head, head, foot], axis=0)
            tiles.append(jnp.exp(dot(left[...], right, ((1,), (0,)), None)).astype(jnp.bfloat16))
        if gate:
            gate()
        terms = []
        for (o, s), tile in zip(places, tiles):
            test = jnp.concatenate([front[l, o, p, s, :split], back[l, s, p, o]], axis=0)
            terms.append(dot(tile, test, ((1,), (0,)), None))
        while len(terms) > 1:
            terms = [a + b for a, b in zip(terms[::2], terms[1::2])] + terms[len(terms) // 2 * 2 :]
        sample[...] += terms[0]

    def landed(ref, recv):
        remote(ref, ref, s_all.at[0], recv, row, col + 1 - 2 * parity).wait_recv()

    def close(n):
        l = origin(n)
        landed(front.at[l, 1 - odd, parity], r_b.at[0, l])
        cross(0, l, 1 - odd).start()
        landed(back.at[l, :most, parity], r_b.at[1, l])
        for k in range(1, half):
            cross(1, l, (spot + k) % half).start()

    def near(n):
        add(origin(n), parity)

    def last(n):
        l = origin(n)
        landed(front.at[l, :, 1 - parity], r_c.at[0, l])
        add(l, 1 - parity, lambda: landed(back.at[l, :, 1 - parity], r_c.at[1, l]))

    def advance(n):
        arrive(n + 1)
        meet(n)

    arrive(0, True)
    each(0, lines - 1, advance)
    meet(lines - 1)
    close(0)

    def finish_line(n):
        close(n)
        near(n - 1)
        last(n - 1)

    each(1, lines, finish_line)
    near(lines - 1)
    last(lines - 1)
    def settle(l):
        for c in range(2):
            pl.when(upward(l))(along(c, l, 0).wait_send)
            pl.when(downward(l))(along(c, l, 1).wait_send)
            leave(hop(c, l) + leaps(c, l))
        leave([cross(0, l, j) for j in range(2)] + [cross(1, l, j) for j in range(half)])


    count = rows * half
    partner = col + 1 - 2 * parity
    total = sample[...]
    index = row * half + spot

    def place(i):
        return lax.div(i, half), 2 * lax.rem(i, half) + parity

    ranks = total.shape[1]

    def cut(ref, low):
        return ref.at[:, ranks // 2 :] if low else ref

    def cuts(ref, low):
        return ref.at[:, :, ranks // 2 :] if low else ref

    def mine_or(make, act):
        for low in range(2):
            pl.when(parity == low)(lambda low=low: act(make(low)))

    def other(make, act):
        for low in range(2):
            pl.when(parity == 1 - low)(lambda low=low: act(make(low)))

    def begin(copy):
        copy.start()

    def got(copy):
        copy.wait_recv()

    def sent(copy):
        copy.wait_send()

    def both(copy):
        copy.wait()

    first, second = total[:, : ranks // 2], total[:, ranks // 2 :]
    square[...] = product(jnp.where(parity == 0, second, first), total, ((0,), (0,))).reshape(square.shape)

    def trade(low):
        return remote(cuts(square, low), cuts(mate, low), s_mate.at[0], r_mate.at[0], row, partner)

    other(trade, begin)
    kept = product(jnp.where(parity == 0, first, second), total, ((0,), (0,))).reshape(square.shape)
    mine[...] = kept
    each(0, lines, settle)
    mine_or(trade, got)
    mine[...] = mine[...] + mate[...]

    def scatter(k):
        there = lax.rem(index + k, count)
        r, c = place(there)
        return lambda low: remote(cut(mine.at[there], low), cut(piece.at[k], low), s_all.at[k], r_piece.at[0], r, c)

    each(1, count, lambda k: mine_or(scatter(k), begin))
    def pieces(low):
        ref = cuts(piece.at[1:], low)
        return remote(ref, ref, s_all.at[0], r_piece.at[0], row, partner)

    mine_or(pieces, got)
    piece[0] = mine[index]
    done[...] = jnp.sum(piece[...], axis=0)
    gram[parity, index] = done[...]

    def collect(k):
        r, c = place(lax.rem(index + k, count))
        return lambda low: remote(cut(done, low), cut(gram.at[parity, index], low), s_all.at[count + k], r_done.at[0], r, c)

    def rest(low):
        ref = cuts(gram.at[low, 1:], low)
        return remote(ref, ref, s_all.at[0], r_done.at[0], row, partner)

    def pass_on(low):
        ref = cuts(gram.at[low], low)
        return remote(ref, ref, s_all.at[0], r_over.at[0], row, partner)

    each(1, count, lambda k: mine_or(collect(k), begin))
    each(1, count, lambda k: mine_or(scatter(k), sent))
    mine_or(rest, got)
    mine_or(pass_on, begin)
    each(1, count, lambda k: mine_or(collect(k), sent))
    mine_or(pass_on, sent)
    other(pass_on, got)
    other(trade, sent)


def far(x):
    return pltpu.with_memory_space_constraint(x, pltpu.HBM)


def sketch_gram(points, tests, rank, boundary, scales, rows, cols):
    local, ranks = tests.shape
    lines, half, count = rows // 2, cols // 2, rows * cols // 2
    lanes = 3 * (8 * ((points.shape[0] + 7) // 8)) + 8
    split = (local - lanes) // 32 * 16
    share = ranks // 2 // count
    f32 = jnp.float32
    dma = pltpu.SemaphoreType.DMA
    wide, most = max(2, half), half - 1
    sample, gram = pl.pallas_call(
        functools.partial(sample_kernel, rows, cols),
        out_shape=(
            jax.ShapeDtypeStruct((local, ranks), f32),
            jax.ShapeDtypeStruct((2, count, share, ranks), f32),
        ),
        in_specs=[HBM, HBM, HBM, SMEM, HBM],
        out_specs=(VMEM, VMEM),
        scratch_shapes=[
            pltpu.VMEM((lines, 2, 2, half, split + lanes, ranks), tests.dtype),
            pltpu.VMEM((lines, half, 2, 2, local - split, ranks), tests.dtype),
            pltpu.VMEM((local, 2 * lanes), tests.dtype),
            pltpu.VMEM(points.shape, f32), pltpu.VMEM((1, local), rank.dtype), pltpu.SMEM(scales.shape, f32), dma((5,)),
            pltpu.VMEM((count, share, ranks), f32),
            pltpu.VMEM((count, share, ranks), f32),
            pltpu.VMEM((count, share, ranks), f32),
            pltpu.VMEM((count, share, ranks), f32),
            pltpu.VMEM((share, ranks), f32),
            dma((max(2 * (lines + 1 + lines * most + lines * max(half, 2 * most) + lines * wide), 2 * count),)),
            dma((2, lines)), dma((2, lines, most)), dma((2, lines)), dma((2, lines)),
            dma((1,)), dma((1,)), dma((1,)), dma((1,)), dma((1,)),
        ],
        compiler_params=pltpu.CompilerParams(
            collective_id=0,
            has_side_effects=True,
            vmem_limit_bytes=2 * rows * cols * (local + lanes) * ranks + 8 * 2**20,
        ),
        name="sketch_gram",
    )(far(points), far(tests), far(rank[None]), boundary, far(scales))
    return sample, gram.reshape(ranks, ranks)


def tree(parts):
    while len(parts) > 1:
        parts = [p + q for p, q in zip(parts[::2], parts[1::2])] + parts[len(parts) // 2 * 2 :]
    return parts[0]


def sixfold(a, b):
    ah, am, al = thirds(a)
    bh, bm, bl = thirds(b)
    return jnp.concatenate([ah, ah, am, ah, al, am], axis=0), jnp.concatenate([bh, bm, bh, bl, bh, bm], axis=0)


def factor_block(a, zero):
    size, wide, width = a.shape[0], 8, 32
    shape = (wide, size)
    lane = lax.broadcasted_iota(jnp.int32, shape, 1)
    line = lax.broadcasted_iota(jnp.int32, shape, 0)

    def spread(x):
        return jnp.broadcast_to(x, shape)

    def column(x, at):
        return jnp.take_along_axis(x, zero + at, axis=1, mode="promise_in_bounds")

    rest = a
    upper, inverse = [], []
    for begin in range(0, size, width):
        end = begin + width
        blocks = [rest[i : i + wide] for i in range(0, width, wide)]
        us, ms = [], []
        marks = [column(blocks[0], begin + u) for u in range(wide)]
        for at in range(begin, end, wide):
            inside = (lane >= at) & (lane < at + wide)
            x = blocks.pop(0)
            z = jnp.where(inside, jnp.where(lane - at == line, 1.0, 0.0), x)
            y = z
            old = [[column(block, at + t) for t in range(wide)] for block in blocks]
            ahead = [column(x, at + wide + u) for u in range(wide)] if blocks else []
            fresh = [column(blocks[0], at + wide + u) for u in range(wide)] if blocks else []
            over, root = jnp.zeros(shape, jnp.float32), jnp.zeros(shape, jnp.float32)
            for s in range(wide):
                pivot = spread(marks[s][s : s + 1])
                inv = 1.0 / pivot
                over = jnp.where(line == s, inv, over)
                root = jnp.where(line == s, pivot, root)
                ratio = marks[s] * inv
                low = jnp.where(line > s, ratio, 0.0)
                both = jnp.where(line == s, 0.0, ratio)
                for u in range(s + 1, wide):
                    marks[u] = marks[u] - both * spread(marks[u][s : s + 1])
                ahead = [c - both * spread(c[s : s + 1]) for c in ahead]
                if s + 1 < wide:
                    x = x - low * spread(x[s : s + 1])
                    y = y - low * spread(y[s : s + 1])
                z = z - both * spread(z[s : s + 1])
            ahead = [c * over for c in ahead]
            marks = [
                f - tree([old[0][t] * spread(c[t : t + 1]) for t in range(wide)]) for f, c in zip(fresh, ahead)
            ]
            z = z * over
            rows = [spread(z[t : t + 1]) for t in range(wide)]
            blocks = [
                jnp.where(inside, 0.0, block) - tree([c * r for c, r in zip(columns, rows)])
                for block, columns in zip(blocks, old)
            ]
            root = lax.rsqrt(root)
            us.append(jnp.where(lane >= at + line, x * root, 0.0))
            ms.append(jnp.where(lane <= at + line, y * root, 0.0))
        u, m = jnp.concatenate(us, axis=0), jnp.concatenate(ms, axis=0)
        upper.append(u)
        inverse.append(m)
        if end < size:
            left, right = sixfold(u, jnp.where(lax.broadcasted_iota(jnp.int32, u.shape, 1) >= end, u, m))
            change = dot(left.T[end:].astype(jnp.bfloat16), right.astype(jnp.bfloat16), ((1,), (0,)), None)
            spot = lax.broadcasted_iota(jnp.int32, change.shape, 1)
            rest = jnp.where((spot >= begin) & (spot < end), 0.0, rest[width:]) - change
    return jnp.concatenate(upper, axis=0), jnp.concatenate(inverse, axis=0)


def product(a, b, dims):
    (i,), (j,) = dims
    ah, am, al = [part.astype(jnp.bfloat16) for part in thirds(a)]
    bh, bm, bl = [part.astype(jnp.bfloat16) for part in thirds(b)]
    return dot(jnp.concatenate([ah, ah, am, ah, al, am], axis=i), jnp.concatenate([bh, bm, bh, bl, bh, bm], axis=j), dims, None)


def finish_kernel(scale, gram, sample, basis, factor):
    half = gram.shape[0] // 2
    head, cross, foot = [part * scale for part in (gram[:half, :half], gram[:half, half:], gram[half:, half:])]
    same = lax.broadcasted_iota(jnp.int32, (half, half), 0) == lax.broadcasted_iota(jnp.int32, (half, half), 1)
    trace = jnp.sum(jnp.sum(jnp.where(same, head + foot, 0.0), axis=0, keepdims=True), axis=1, keepdims=True)
    shift = jnp.where(same, (0.05 / half) * trace, 0.0)
    zero = (head[:8] * 0.0).astype(jnp.int32)
    up, low = factor_block(head + shift, zero)
    lift = product(low, cross, ((1,), (0,)))
    up2, low2 = factor_block(foot + shift - product(lift.T, lift, ((1,), (0,))), zero)
    first = product(sample[:, :half], low, ((1,), (1,)))
    rest = sample[:, half:] - product(first, lift, ((1,), (0,)))
    basis[:, :half] = first
    basis[:, half:] = product(rest, low2, ((1,), (1,)))
    factor[:half, :half] = up.T
    factor[:half, half:] = jnp.zeros((half, half), jnp.float32)
    factor[half:, :half] = lift.T
    factor[half:, half:] = up2.T


def finish(gram, sample, everyone):
    return pl.pallas_call(
        functools.partial(finish_kernel, 1.0 / everyone),
        out_shape=(
            jax.ShapeDtypeStruct(sample.shape, jnp.float32),
            jax.ShapeDtypeStruct(gram.shape, jnp.float32),
        ),
        in_specs=[VMEM, VMEM],
        out_specs=(VMEM, VMEM),
        compiler_params=pltpu.CompilerParams(vmem_limit_bytes=8 * 2**20),
        name="finish",
    )(gram, sample)


def body(rows, cols, points, sketch, rank, boundary, scales):
    sample, gram = sketch_gram(points, sketch, rank, boundary, scales, rows, cols)
    return finish(gram, sample, rows * cols * points.shape[1])


def solution(mesh):
    placed = (P(None, ("row", "col")), P(("row", "col"), None), P(("row", "col")), P(), P())
    return jax.shard_map(
        functools.partial(body, mesh.shape["row"], mesh.shape["col"]),
        mesh=mesh,
        in_specs=placed,
        out_specs=(P(("row", "col"), None), P()),
        check_vma=False,
    )
```
